512 devices in a mesh: member: 32 (over z, x), wave: 16 (over y, core).
Axes of the slice: x: 4, y: 8, z: 8, core: 2. Of those that a mesh axis runs over, the one named last changes fastest.
Arguments:
- state: float32 [32, 128, 32, 640], P('member', 'wave'), may hold values from -6 to 6
- legendre: bfloat16 [128, 640, 640], P('wave'), may hold values from -0.25 to 0.25
- lat_weights: float32 [640], replicated, may hold values from 0.5 to 2
- region: int32 [4], replicated, may hold values from 0 to 2560, as said below
- sources: int32 [32], replicated, may hold values from 0 to 31, as said below
Outputs:
- new_states: float32 [32, 128, 32, 640], P('member', 'wave')
- scores: float32 [32], P('member')
The draws below stay inside these ranges and needn't reach their ends.
Inputs may be any that keep to these rules, and one draw needn't show every extreme that they name: region[0] < region[1] bound the latitudes and region[2] < region[3] the longitudes of the region; each band covers at least half of its grid dimension; the longitude band ends at the last longitude, region[3] = 2560. `sources`: some member is the source of at least 8 slots.
All inputs are finite; a program needn't handle non-finite values.
Results may differ from the reference program's by a relative error of at most 0.0059.
Values may be sent and summed in bfloat16 or wider, within the bound.
No kernel may reach another device: no remote copies, remote signals or barrier semaphores. Data moves between devices by JAX's collectives and lax.ppermute only.
A program may use at most 128 MiB of HBM per device.

```python
import math
import jax
import jax.numpy as jnp
from jax import lax

NDEG = 640
NLAT = 640
NLON = 2560
LEV = 8
MW = 128
ROWS = 32
MEMBERS = 32


def draw_region(key, part):
    keys = jax.random.split(jax.random.fold_in(key, 11), 3)
    lat_low = jax.random.randint(keys[0], (), 0, NLAT // 8)
    lat_high = NLAT - jax.random.randint(keys[1], (), 0, NLAT // 8)
    lon_low = jax.random.randint(keys[2], (), 0, NLON // 2)
    lon_high = jnp.int32(NLON) + 0 * lon_low
    return jnp.stack([lat_low, lat_high, lon_low, lon_high]).astype(jnp.int32)


def draw_sources(key, part):
    keys = jax.random.split(jax.random.fold_in(key, 7), 2)
    picks = jax.random.randint(keys[0], (MEMBERS,), 0, MEMBERS)
    favored = jax.random.randint(keys[1], (), 0, MEMBERS)
    slots = jnp.arange(MEMBERS)
    offset = (slots - favored) % MEMBERS
    picks = jnp.where((offset >= 1) & (offset <= MEMBERS // 4), favored, picks)
    picks = jnp.where(offset == MEMBERS // 4 + 1, 0, picks)
    picks = jnp.where(offset == MEMBERS // 4 + 2, MEMBERS - 1, picks)
    picks = jnp.where(offset == MEMBERS // 2 + 1, (favored + 1) % MEMBERS, picks)
    return picks.astype(jnp.int32)


def levels(key, extent, pieces, smallest, high):
    def one(dim, parts):
        steps = jax.random.uniform(jax.random.fold_in(jax.random.fold_in(key, 6), dim), (parts,), jnp.float32, smallest / len(pieces), high / len(pieces))
        return jnp.repeat(jnp.exp(steps), extent[dim] // parts).reshape((-1,) + (1,) * (len(extent) - dim - 1))

    loudness = one(*pieces[0])
    for cut in pieces[1:]:
        loudness = loudness * one(*cut)
    return loudness


def noise(rng, extent, spread, reach, pieces=(), dtype=jnp.bfloat16):
    result = spread * jax.random.normal(rng, extent, jnp.float32)
    if pieces:
        result = result * levels(rng, extent, pieces, -0.22, 0.18)
    return jnp.clip(result, -reach, reach).astype(dtype)


def setup_inputs(seed: int = 0) -> dict:
    key_list = jax.random.split(jax.random.key(seed), 6)
    state = noise(key_list[0], (MEMBERS, MW, ROWS, NDEG), 1.0, 6.0, ((0, 32), (1, 16)), jnp.float32)
    legendre = noise(key_list[1], (MW, NDEG, NLAT), NDEG ** -0.5, 0.25, ((0, 16),))
    lat_weights = jnp.clip(jnp.exp(jax.random.uniform(key_list[2], (NLAT,), jnp.float32, math.log(0.5), math.log(2.0))), 0.5, 2.0)
    region = draw_region(jax.random.fold_in(key_list[5], 71), 0)
    sources = draw_sources(jax.random.fold_in(key_list[5], 71), 0)
    return dict(state=state, legendre=legendre, lat_weights=lat_weights, region=region, sources=sources)


advect_rate = 2.0


def fourier_table(waves_total, points):
    wave_index = lax.broadcasted_iota(jnp.int32, (waves_total, points), 0)
    column_index = lax.broadcasted_iota(jnp.int32, (waves_total, points), 1)
    angles = ((wave_index * column_index) % points).astype(jnp.float32) * (2.0 * jnp.pi / points)
    return jnp.stack([jnp.cos(angles), -jnp.sin(angles)], axis=1).astype(jnp.bfloat16)


def advance(state_one, legendre, lat_weights, region, fourier):
    spectral = lax.optimization_barrier(state_one.astype(jnp.bfloat16)).astype(jnp.float32)
    legendre_wide = legendre.astype(jnp.float32)
    fourier_wide = fourier.astype(jnp.float32)
    fourier_coef = jnp.einsum('mrn,mnl->mrl', spectral, legendre_wide).astype(jnp.bfloat16)
    fourier_coef = lax.optimization_barrier(fourier_coef).astype(jnp.float32).reshape(MW, 2, 2 * LEV, NLAT)
    gridded = (2.0 * MW) ** -0.5 * jnp.einsum('mckl,mcx->klx', fourier_coef, fourier_wide)
    wind_grid = gridded[:LEV]
    temper_grid = gridded[LEV:]
    weights_column = lat_weights[None, :, None]
    fluxes = jnp.concatenate([0.5 * wind_grid * wind_grid, wind_grid * temper_grid], axis=0) * weights_column
    fluxes = lax.optimization_barrier(fluxes.astype(jnp.bfloat16)).astype(jnp.float32)
    lat_index = lax.broadcasted_iota(jnp.int32, (NLAT, 1), 0)
    lon_index = lax.broadcasted_iota(jnp.int32, (1, NLON), 1)
    lat_inside = (lat_index >= region[0]) & (lat_index < region[1])
    in_region = lat_inside & (lon_index >= region[2]) & (lon_index < region[3])
    lowest = temper_grid[LEV - 1]
    region_total = jnp.sum(jnp.where(in_region, lat_weights[:, None] * lowest * lowest, jnp.float32(0.0)))
    region_weight = jnp.sum(jnp.where(lat_inside[:, 0], lat_weights, jnp.float32(0.0))) * (region[3] - region[2]).astype(jnp.float32)
    score_value = region_total / region_weight
    flux_coef = (NLON ** -0.5 * jnp.einsum('klx,mcx->mckl', fluxes, fourier_wide)).astype(jnp.bfloat16)
    flux_coef = lax.optimization_barrier(flux_coef).astype(jnp.float32)
    tendency = jnp.einsum('mckl,mnl->mckn', flux_coef, legendre_wide)
    wave_ids = lax.broadcasted_iota(jnp.int32, (MW, 1, 1), 0).astype(jnp.float32)
    advection = advect_rate * wave_ids / MW
    degree_ids = lax.broadcasted_iota(jnp.int32, (1, 1, NDEG), 2).astype(jnp.float32)
    damping = 1.0 + ((degree_ids + 1.0) / NDEG) ** 2
    spectral_split = state_one.reshape(MW, 2, 2 * LEV, NDEG)
    real_part = (spectral_split[:, 0] + advection * tendency[:, 1]) / damping
    imag_part = (spectral_split[:, 1] - advection * tendency[:, 0]) / damping
    stepped = jnp.stack([real_part, imag_part], axis=1).reshape(MW, ROWS, NDEG)
    return stepped, score_value


def reference(state, legendre, lat_weights, region, sources):
    fourier = fourier_table(MW, NLON)
    stepped, scores = lax.map(lambda single: advance(single, legendre, lat_weights, region, fourier), state)
    new_states = jnp.take(stepped, sources, axis=0)
    return new_states, scores
```

```python
import functools

import jax
import jax.numpy as jnp
from jax import lax
from jax.experimental import pallas as pl
from jax.experimental.pallas import tpu as pltpu
from jax.sharding import PartitionSpec as P

NLON = 2560
LANES = 128
COLUMNS = 256

advect_rate = 2.0


def fourier_table(waves_total, points):
    row = lax.broadcasted_iota(jnp.int32, (2 * waves_total, points), 0)
    column = lax.broadcasted_iota(jnp.int32, (2 * waves_total, points), 1)
    steps = ((row // 2) * column + (row % 2) * (points // 4)) % points
    angles = steps.astype(jnp.float32) * (2.0 * jnp.pi / points)
    return jnp.cos(angles).astype(jnp.bfloat16)


def put_rows(tiles_ref, where, values):
    for tile in range(tiles_ref.shape[0]):
        tiles_ref[tile, where, :] = values[:, tile * LANES : (tile + 1) * LANES]


def get_rows(tiles_ref, where):
    return jnp.concatenate([tiles_ref[tile, where, :] for tile in range(tiles_ref.shape[0])], axis=1)


def to_latitudes(levels, state_ref, legendre_ref, out_ref, rows_ref):
    step = pl.program_id(0)
    rows = state_ref.shape[1]
    first = pl.multiple_of(step * rows, rows)
    put_rows(
        rows_ref,
        pl.ds(first, rows),
        jnp.dot(
            state_ref[0].astype(jnp.bfloat16), legendre_ref[0], preferred_element_type=jnp.float32
        ),
    )

    @pl.when(step == pl.num_programs(0) - 1)
    def _():
        count = out_ref.shape[1]
        width = out_ref.shape[2]
        half = width // 2
        left = lax.broadcasted_iota(jnp.int32, (count, width), 1) < half
        for level in range(levels):
            wind = get_rows(rows_ref, pl.ds(level, count, stride=2 * levels))
            temper = get_rows(rows_ref, pl.ds(levels + level, count, stride=2 * levels))
            low = jnp.where(left, wind, pltpu.roll(temper, half, 1))
            high = jnp.where(left, pltpu.roll(wind, half, 1), temper)
            out_ref[2 * level] = low.astype(jnp.bfloat16)
            out_ref[2 * level + 1] = high.astype(jnp.bfloat16)


def on_grid(
    synthesis_scale,
    analysis_scale,
    info_ref,
    coef_ref,
    fourier_ref,
    weights_ref,
    out_ref,
    score_ref,
    turned_ref,
    total_ref,
    region_ref,
):
    points = fourier_ref.shape[1]
    lats = weights_ref.shape[0]
    turned_ref[...] = coef_ref[...].T
    total_ref[...] = jnp.zeros_like(total_ref)
    region_ref[...] = jnp.zeros_like(region_ref)
    weights = weights_ref[...]
    for part in range(points // COLUMNS):
        table = fourier_ref[:, part * COLUMNS : (part + 1) * COLUMNS]
        grid = synthesis_scale * jnp.dot(
            turned_ref[...], table, preferred_element_type=jnp.float32
        )
        wind, temper = grid[:lats], grid[lats:]
        weighted = wind * weights
        total_ref[:lats] += lax.dot_general(
            (0.5 * wind * weighted).astype(jnp.bfloat16),
            table,
            (((1,), (1,)), ((), ())),
            preferred_element_type=jnp.float32,
        )
        total_ref[lats:] += lax.dot_general(
            (weighted * temper).astype(jnp.bfloat16),
            table,
            (((1,), (1,)), ((), ())),
            preferred_element_type=jnp.float32,
        )
        column = part * COLUMNS + lax.broadcasted_iota(jnp.int32, (1, COLUMNS), 1)
        inside = (column >= info_ref[2]) & (column < info_ref[3])
        region_ref[...] += jnp.where(inside, temper * temper, 0.0)
    lat = info_ref[4] + lax.broadcasted_iota(jnp.int32, (lats, 1), 0)
    lat_inside = (lat >= info_ref[0]) & (lat < info_ref[1]) & (info_ref[5] == 1)
    score_ref[...] = jnp.sum(
        jnp.where(lat_inside, weights, 0.0) * jnp.sum(region_ref[...], axis=1, keepdims=True),
        axis=0,
        keepdims=True,
    )
    score = jnp.broadcast_to(score_ref[...], (out_ref.shape[0], LANES))
    high = score.astype(jnp.bfloat16).astype(jnp.float32)
    middle = (score - high).astype(jnp.bfloat16).astype(jnp.float32)
    low = score - high - middle
    lane = lax.broadcasted_iota(jnp.int32, score.shape, 1)
    parts = jnp.where(lane == 0, high, jnp.where(lane == 1, middle, jnp.where(lane == 2, low, 0.0)))
    out_ref[:, 2 * lats :] = parts.astype(jnp.bfloat16)
    out_ref[:, : 2 * lats] = (analysis_scale * total_ref[...]).T.astype(jnp.bfloat16)


def to_degrees(
    levels,
    waves_total,
    info_ref,
    coef_ref,
    legendre_ref,
    state_ref,
    lat_weights_ref,
    out_ref,
    scores_ref,
    wide_ref,
):
    step = pl.program_id(0)
    steps = pl.num_programs(0)
    owners, kept, _ = coef_ref.shape
    lats = lat_weights_ref.shape[1]
    half = lats // 2

    @pl.when(step == 0)
    def _():
        parts = jnp.zeros((1, LANES), jnp.float32)
        for owner in range(owners):
            put_rows(
                wide_ref,
                pl.ds(owner * kept, kept),
                coef_ref[owner][:, :lats].astype(jnp.float32),
            )
            parts += coef_ref[owner][0:1, lats:].astype(jnp.float32)
        lat = lax.broadcasted_iota(jnp.int32, (1, lats), 1)
        inside = (lat >= info_ref[0]) & (lat < info_ref[1])
        weight = jnp.sum(jnp.where(inside, lat_weights_ref[...], 0.0), axis=1, keepdims=True)
        columns = (info_ref[3] - info_ref[2]).astype(jnp.float32)
        scores_ref[...] = jnp.sum(parts, axis=1, keepdims=True) / (weight * columns)

    left = lax.broadcasted_iota(jnp.int32, (levels, lats), 1) < half
    rows = []
    for part in range(2):
        first = get_rows(wide_ref, pl.ds(2 * step + part, levels, stride=2 * kept))
        second = get_rows(wide_ref, pl.ds(kept + 2 * step + part, levels, stride=2 * kept))
        rows.append(jnp.where(left, first, pltpu.roll(second, half, 1)))
        rows.append(jnp.where(left, pltpu.roll(first, half, 1), second))
    tendency = lax.dot_general(
        jnp.concatenate(rows, axis=0).astype(jnp.bfloat16),
        legendre_ref[0],
        (((1,), (1,)), ((), ())),
        preferred_element_type=jnp.float32,
    )
    wave = (info_ref[6] * steps + step).astype(jnp.float32)
    advection = advect_rate * wave / waves_total
    degrees = tendency.shape[1]
    degree = lax.broadcasted_iota(jnp.int32, (1, degrees), 1).astype(jnp.float32)
    damping = 1.0 + ((degree + 1.0) / degrees) ** 2
    middle = 2 * levels
    out_ref[0, :middle] = (
        (state_ref[0, :middle] + advection * tendency[middle:]) / damping
    ).astype(jnp.bfloat16)
    out_ref[0, middle:] = (
        (state_ref[0, middle:] - advection * tendency[:middle]) / damping
    ).astype(jnp.bfloat16)


def pick(sources_ref, pieces_ref, out_ref):
    for slot in range(out_ref.shape[0]):
        out_ref[slot] = pieces_ref[sources_ref[slot]]


def on_device(state, legendre, lat_weights, region, sources):
    wave_count = lax.axis_size("wave")
    member_count = lax.axis_size("member")
    waves_local, degrees, latitudes = legendre.shape
    waves_total = waves_local * wave_count
    state_rows = state.shape[2]
    levels = state_rows // 4
    half = latitudes // 2
    kept = 2 * waves_local
    wave = lax.axis_index("wave")
    level = wave // 2
    lat_start = (wave % 2) * half
    spectral = state[0]
    vmem = functools.partial(pltpu.CompilerParams, vmem_limit_bytes=32 << 20)

    coef = pl.pallas_call(
        functools.partial(to_latitudes, levels),
        grid=(waves_local,),
        in_specs=[
            pl.BlockSpec((1, state_rows, degrees), lambda i: (i, 0, 0)),
            pl.BlockSpec((1, degrees, latitudes), lambda i: (i, 0, 0)),
        ],
        out_specs=pl.BlockSpec((wave_count, kept, latitudes), lambda i: (0, 0, 0)),
        out_shape=jax.ShapeDtypeStruct((wave_count, kept, latitudes), jnp.bfloat16),
        scratch_shapes=[pltpu.VMEM((latitudes // LANES, waves_local * state_rows, LANES), jnp.float32)],
        compiler_params=vmem(),
        name="to_latitudes",
    )(spectral, legendre)
    coef = lax.all_to_all(coef, "wave", split_axis=0, concat_axis=0, tiled=True)

    fourier = fourier_table(waves_total, NLON)
    info = jnp.concatenate(
        [
            region,
            jnp.stack([lat_start, (level == levels - 1).astype(jnp.int32), wave]).astype(jnp.int32),
        ]
    )
    weights = lax.dynamic_slice_in_dim(lat_weights, lat_start, half).reshape(half, 1)
    whole = pl.BlockSpec(memory_space=pltpu.VMEM)
    scalars = pl.BlockSpec(memory_space=pltpu.SMEM)
    width = latitudes + LANES
    flux_coef, _ = pl.pallas_call(
        functools.partial(on_grid, (2.0 * waves_total) ** (-0.5), NLON ** (-0.5)),
        in_specs=[scalars, whole, whole, whole],
        out_specs=[whole, whole],
        out_shape=[
            jax.ShapeDtypeStruct((2 * waves_total, width), jnp.bfloat16),
            jax.ShapeDtypeStruct((1, 1), jnp.float32),
        ],
        scratch_shapes=[
            pltpu.VMEM((latitudes, 2 * waves_total), jnp.bfloat16),
            pltpu.VMEM((latitudes, 2 * waves_total), jnp.float32),
            pltpu.VMEM((half, COLUMNS), jnp.float32),
        ],
        compiler_params=vmem(),
        name="on_grid",
    )(info, coef.reshape(2 * waves_total, latitudes), fourier, weights)
    flux_coef = lax.all_to_all(
        flux_coef.reshape(wave_count, kept, width), "wave", split_axis=0, concat_axis=0, tiled=True
    )

    stepped, scores = pl.pallas_call(
        functools.partial(to_degrees, levels, waves_total),
        grid=(waves_local,),
        in_specs=[
            scalars,
            pl.BlockSpec((wave_count, kept, width), lambda i: (0, 0, 0)),
            pl.BlockSpec((1, degrees, latitudes), lambda i: (i, 0, 0)),
            pl.BlockSpec((1, state_rows, degrees), lambda i: (i, 0, 0)),
            pl.BlockSpec((1, latitudes), lambda i: (0, 0)),
        ],
        out_specs=[
            pl.BlockSpec((1, state_rows, degrees), lambda i: (i, 0, 0)),
            pl.BlockSpec((1, 1), lambda i: (0, 0)),
        ],
        out_shape=[
            jax.ShapeDtypeStruct((waves_local, state_rows, degrees), jnp.bfloat16),
            jax.ShapeDtypeStruct((1, 1), jnp.float32),
        ],
        scratch_shapes=[pltpu.VMEM((latitudes // LANES, wave_count * kept, LANES), jnp.float32)],
        compiler_params=vmem(),
        name="to_degrees",
    )(info, flux_coef, legendre, spectral, lat_weights.reshape(1, latitudes))

    piece_rows = waves_local * state_rows // member_count
    pieces = lax.all_to_all(
        stepped.reshape(member_count, piece_rows, degrees),
        "member",
        split_axis=0,
        concat_axis=0,
        tiled=True,
    )
    picked = pl.pallas_call(
        pick,
        in_specs=[scalars, whole],
        out_specs=whole,
        out_shape=jax.ShapeDtypeStruct(pieces.shape, jnp.bfloat16),
        compiler_params=vmem(),
        name="pick",
    )(sources, pieces)
    cloned = lax.all_to_all(picked, "member", split_axis=0, concat_axis=0, tiled=True)
    cloned = cloned.reshape(1, waves_local, state_rows, degrees).astype(jnp.float32)
    return (cloned, scores.reshape(1))


def solution(mesh):
    in_specs = (P("member", "wave", None, None), P("wave", None, None), P(), P(), P())
    out_specs = (P("member", "wave", None, None), P("member"))
    return jax.shard_map(
        on_device, mesh=mesh, in_specs=in_specs, out_specs=out_specs, check_vma=False
    )
```

```python
import functools

import jax
import jax.numpy as jnp
from jax import lax
from jax.experimental import pallas as pl
from jax.experimental.pallas import tpu as pltpu
from jax.sharding import PartitionSpec as P

NLON = 2560
LANES = 128
COLUMNS = 256

advect_rate = 2.0


def fourier_table(waves_total, points):
    def angles(columns, stride, shift):
        row = lax.broadcasted_iota(jnp.int32, (2 * waves_total, columns), 0)
        column = lax.broadcasted_iota(jnp.int32, (2 * waves_total, columns), 1)
        steps = ((row >> 1) * (column * stride) + (row & 1) * shift) % points
        return steps.astype(jnp.float32) * (2.0 * jnp.pi / points)

    coarse = angles(points // LANES, LANES, points // 4)
    fine = angles(LANES, 1, 0)
    terms = lax.optimization_barrier(
        (jnp.cos(coarse), jnp.sin(coarse), jnp.cos(fine), jnp.sin(fine))
    )
    cos_coarse, sin_coarse = (term[:, :, None] for term in terms[:2])
    cos_fine, sin_fine = (term[:, None, :] for term in terms[2:])
    table = cos_coarse * cos_fine - sin_coarse * sin_fine
    return table.astype(jnp.bfloat16).reshape(2 * waves_total, points)


def put_rows(tiles_ref, where, values):
    for tile in range(tiles_ref.shape[0]):
        tiles_ref[tile, where, :] = values[:, tile * LANES : (tile + 1) * LANES]


def get_rows(tiles_ref, where):
    return jnp.concatenate([tiles_ref[tile, where, :] for tile in range(tiles_ref.shape[0])], axis=1)


def fetch(waves, *routes):
    copies = [
        [pltpu.make_async_copy(far.at[wave], near.at[wave], sems.at[wave]) for far, near, sems in routes]
        for wave in range(waves)
    ]
    for group in copies:
        for copy in group:
            copy.start()
    return copies


def to_latitudes(
    levels, state_hbm, legendre_hbm, out_ref, legendre_ref, state_ref, rows_ref, state_sems, legendre_sems
):
    waves, rows, _ = state_hbm.shape
    copies = fetch(waves, (state_hbm, state_ref, state_sems), (legendre_hbm, legendre_ref, legendre_sems))
    for wave in range(waves):
        for copy in copies[wave]:
            copy.wait()
        put_rows(
            rows_ref,
            pl.ds(wave * rows, rows),
            jnp.dot(
                state_ref[wave].astype(jnp.bfloat16),
                legendre_ref[wave],
                preferred_element_type=jnp.float32,
            ),
        )
    _, count, width = out_ref.shape
    half = width // 2
    left = lax.broadcasted_iota(jnp.int32, (count, width), 1) < half
    for level in range(levels):
        wind = get_rows(rows_ref, pl.ds(level, count, stride=2 * levels))
        temper = get_rows(rows_ref, pl.ds(levels + level, count, stride=2 * levels))
        low = jnp.where(left, wind, pltpu.roll(temper, half, 1))
        high = jnp.where(left, pltpu.roll(wind, half, 1), temper)
        out_ref[2 * level] = low.astype(jnp.bfloat16)
        out_ref[2 * level + 1] = high.astype(jnp.bfloat16)


def on_grid(
    synthesis_scale,
    analysis_scale,
    info_ref,
    coef_ref,
    fourier_ref,
    weights_ref,
    out_ref,
    score_ref,
    turned_ref,
    total_ref,
    region_ref,
):
    points = fourier_ref.shape[1]
    lats = weights_ref.shape[0]
    turned_ref[...] = coef_ref[...].T
    total_ref[...] = jnp.zeros_like(total_ref)
    region_ref[...] = jnp.zeros_like(region_ref)
    weights = weights_ref[...]
    for part in range(points // COLUMNS):
        table = fourier_ref[:, part * COLUMNS : (part + 1) * COLUMNS]
        grid = synthesis_scale * jnp.dot(
            turned_ref[...], table, preferred_element_type=jnp.float32
        )
        wind, temper = grid[:lats], grid[lats:]
        weighted = wind * weights
        total_ref[:lats] += lax.dot_general(
            (0.5 * wind * weighted).astype(jnp.bfloat16),
            table,
            (((1,), (1,)), ((), ())),
            preferred_element_type=jnp.float32,
        )
        total_ref[lats:] += lax.dot_general(
            (weighted * temper).astype(jnp.bfloat16),
            table,
            (((1,), (1,)), ((), ())),
            preferred_element_type=jnp.float32,
        )
        column = part * COLUMNS + lax.broadcasted_iota(jnp.int32, (1, COLUMNS), 1)
        inside = (column >= info_ref[2]) & (column < info_ref[3])
        region_ref[...] += jnp.where(inside, temper * temper, 0.0)
    lat = info_ref[4] + lax.broadcasted_iota(jnp.int32, (lats, 1), 0)
    lat_inside = (lat >= info_ref[0]) & (lat < info_ref[1]) & (info_ref[5] == 1)
    score_ref[...] = jnp.sum(
        jnp.where(lat_inside, weights, 0.0) * jnp.sum(region_ref[...], axis=1, keepdims=True),
        axis=0,
        keepdims=True,
    )
    score = jnp.broadcast_to(score_ref[...], (out_ref.shape[0], LANES))
    high = score.astype(jnp.bfloat16).astype(jnp.float32)
    middle = (score - high).astype(jnp.bfloat16).astype(jnp.float32)
    low = score - high - middle
    lane = lax.broadcasted_iota(jnp.int32, score.shape, 1)
    parts = jnp.where(lane == 0, high, jnp.where(lane == 1, middle, jnp.where(lane == 2, low, 0.0)))
    out_ref[:, 2 * lats :] = parts.astype(jnp.bfloat16)
    out_ref[:, : 2 * lats] = (analysis_scale * total_ref[...]).T.astype(jnp.bfloat16)


def to_degrees(
    levels,
    waves_total,
    info_ref,
    coef_ref,
    legendre_hbm,
    state_hbm,
    lat_weights_ref,
    out_ref,
    scores_ref,
    legendre_ref,
    state_ref,
    wide_ref,
    state_sems,
    legendre_sems,
):
    copies = fetch(
        state_hbm.shape[0], (state_hbm, state_ref, state_sems), (legendre_hbm, legendre_ref, legendre_sems)
    )
    owners, kept, _ = coef_ref.shape
    waves, degrees, lats = legendre_ref.shape
    half = lats // 2
    parts = jnp.zeros((1, LANES), jnp.float32)
    for owner in range(owners):
        put_rows(
            wide_ref,
            pl.ds(owner * kept, kept),
            coef_ref[owner][:, :lats].astype(jnp.float32),
        )
        parts += coef_ref[owner][0:1, lats:].astype(jnp.float32)
    lat = lax.broadcasted_iota(jnp.int32, (1, lats), 1)
    inside = (lat >= info_ref[0]) & (lat < info_ref[1])
    weight = jnp.sum(jnp.where(inside, lat_weights_ref[...], 0.0), axis=1, keepdims=True)
    columns = (info_ref[3] - info_ref[2]).astype(jnp.float32)
    scores_ref[...] = jnp.sum(parts, axis=1, keepdims=True) / (weight * columns)

    degree = lax.broadcasted_iota(jnp.int32, (1, degrees), 1).astype(jnp.float32)
    damping = 1.0 + ((degree + 1.0) / degrees) ** 2
    left = lax.broadcasted_iota(jnp.int32, (levels, lats), 1) < half
    middle = 2 * levels
    for wave in range(waves):
        rows = []
        for part in range(2):
            first = get_rows(wide_ref, pl.ds(2 * wave + part, levels, stride=2 * kept))
            second = get_rows(wide_ref, pl.ds(kept + 2 * wave + part, levels, stride=2 * kept))
            rows.append(jnp.where(left, first, pltpu.roll(second, half, 1)))
            rows.append(jnp.where(left, pltpu.roll(first, half, 1), second))
        for copy in copies[wave]:
            copy.wait()
        tendency = lax.dot_general(
            jnp.concatenate(rows, axis=0).astype(jnp.bfloat16),
            legendre_ref[wave],
            (((1,), (1,)), ((), ())),
            preferred_element_type=jnp.float32,
        )
        global_wave = (info_ref[6] * waves + wave).astype(jnp.float32)
        advection = advect_rate * global_wave / waves_total
        out_ref[wave, :middle] = (
            (state_ref[wave, :middle] + advection * tendency[middle:]) / damping
        ).astype(jnp.bfloat16)
        out_ref[wave, middle:] = (
            (state_ref[wave, middle:] - advection * tendency[:middle]) / damping
        ).astype(jnp.bfloat16)


def pick(sources_ref, pieces_ref, out_ref):
    for slot in range(out_ref.shape[0]):
        out_ref[slot] = pieces_ref[sources_ref[slot]]


def on_device(state, legendre, lat_weights, region, sources):
    wave_count = lax.axis_size("wave")
    member_count = lax.axis_size("member")
    waves_local, degrees, latitudes = legendre.shape
    waves_total = waves_local * wave_count
    state_rows = state.shape[2]
    levels = state_rows // 4
    half = latitudes // 2
    kept = 2 * waves_local
    wave = lax.axis_index("wave")
    level = wave // 2
    lat_start = (wave % 2) * half
    spectral = state[0]
    small = pltpu.CompilerParams(vmem_limit_bytes=32 << 20)

    whole = pl.BlockSpec(memory_space=pltpu.VMEM)
    scalars = pl.BlockSpec(memory_space=pltpu.SMEM)
    stay = pl.BlockSpec(memory_space=pltpu.HBM)
    large = pltpu.CompilerParams(vmem_limit_bytes=58 << 20)
    near = [
        pltpu.VMEM(legendre.shape, jnp.bfloat16),
        pltpu.VMEM(spectral.shape, jnp.float32),
    ]
    arrivals = [pltpu.SemaphoreType.DMA((waves_local,)), pltpu.SemaphoreType.DMA((waves_local,))]
    coef = pl.pallas_call(
        functools.partial(to_latitudes, levels),
        in_specs=[stay, stay],
        out_specs=whole,
        out_shape=jax.ShapeDtypeStruct((wave_count, kept, latitudes), jnp.bfloat16),
        scratch_shapes=[
            *near,
            pltpu.VMEM((latitudes // LANES, waves_local * state_rows, LANES), jnp.float32),
            *arrivals,
        ],
        compiler_params=large,
        name="to_latitudes",
    )(spectral, legendre)
    coef = lax.all_to_all(coef, "wave", split_axis=0, concat_axis=0, tiled=True)

    fourier = fourier_table(waves_total, NLON)
    info = jnp.concatenate(
        [
            region,
            jnp.stack([lat_start, (level == levels - 1).astype(jnp.int32), wave]).astype(jnp.int32),
        ]
    )
    weights = lax.dynamic_slice_in_dim(lat_weights, lat_start, half).reshape(half, 1)
    width = latitudes + LANES
    flux_coef, _ = pl.pallas_call(
        functools.partial(on_grid, (2.0 * waves_total) ** (-0.5), NLON ** (-0.5)),
        in_specs=[scalars, whole, whole, whole],
        out_specs=[whole, whole],
        out_shape=[
            jax.ShapeDtypeStruct((2 * waves_total, width), jnp.bfloat16),
            jax.ShapeDtypeStruct((1, 1), jnp.float32),
        ],
        scratch_shapes=[
            pltpu.VMEM((latitudes, 2 * waves_total), jnp.bfloat16),
            pltpu.VMEM((latitudes, 2 * waves_total), jnp.float32),
            pltpu.VMEM((half, COLUMNS), jnp.float32),
        ],
        compiler_params=small,
        name="on_grid",
    )(info, coef.reshape(2 * waves_total, latitudes), fourier, weights)
    lat_row, flux_coef = lax.optimization_barrier((lat_weights.reshape(1, latitudes), flux_coef))
    flux_coef = lax.all_to_all(
        flux_coef.reshape(wave_count, kept, width), "wave", split_axis=0, concat_axis=0, tiled=True
    )

    stepped, scores = pl.pallas_call(
        functools.partial(to_degrees, levels, waves_total),
        in_specs=[scalars, whole, stay, stay, whole],
        out_specs=[whole, whole],
        out_shape=[
            jax.ShapeDtypeStruct((waves_local, state_rows, degrees), jnp.bfloat16),
            jax.ShapeDtypeStruct((1, 1), jnp.float32),
        ],
        scratch_shapes=[
            *near,
            pltpu.VMEM((latitudes // LANES, wave_count * kept, LANES), jnp.float32),
            *arrivals,
        ],
        compiler_params=large,
        name="to_degrees",
    )(info, flux_coef, legendre, spectral, lat_row)

    piece_rows = waves_local * state_rows // member_count
    pieces = lax.all_to_all(
        stepped.reshape(member_count, piece_rows, degrees),
        "member",
        split_axis=0,
        concat_axis=0,
        tiled=True,
    )
    picked = pl.pallas_call(
        pick,
        in_specs=[scalars, whole],
        out_specs=whole,
        out_shape=jax.ShapeDtypeStruct(pieces.shape, jnp.bfloat16),
        compiler_params=small,
        name="pick",
    )(sources, pieces)
    cloned = lax.all_to_all(picked, "member", split_axis=0, concat_axis=0, tiled=True)
    cloned = cloned.reshape(1, waves_local, state_rows, degrees).astype(jnp.float32)
    return (cloned, scores.reshape(1))


def solution(mesh):
    in_specs = (P("member", "wave", None, None), P("wave", None, None), P(), P(), P())
    out_specs = (P("member", "wave", None, None), P("member"))
    return jax.shard_map(
        on_device, mesh=mesh, in_specs=in_specs, out_specs=out_specs, check_vma=False
    )
```

```python
import functools

import jax
import jax.numpy as jnp
from jax import lax
from jax.experimental import pallas as pl
from jax.experimental.pallas import tpu as pltpu
from jax.sharding import PartitionSpec as P

NLON = 2560
LANES = 128
COLUMNS = 256
AHEAD = 4

advect_rate = 2.0


def put_rows(tiles_ref, first_tile, where, values):
    for tile in range(values.shape[1] // LANES):
        tiles_ref[first_tile + tile, where, :] = values[:, tile * LANES : (tile + 1) * LANES]


def get_rows(tiles_ref, first_tile, tiles, where):
    return jnp.concatenate([tiles_ref[first_tile + tile, where, :] for tile in range(tiles)], axis=1)


def routes(waves, *pairs):
    copies = [
        [pltpu.make_async_copy(far.at[wave], near.at[wave], sems.at[wave]) for far, near, sems in pairs]
        for wave in range(waves)
    ]
    for group in copies[:AHEAD]:
        for copy in group:
            copy.start()
    return copies


def arrive(copies, wave):
    for copy in copies[wave]:
        copy.wait()
    for copy in copies[wave + AHEAD] if wave + AHEAD < len(copies) else ():
        copy.start()


def turns(row_steps, column_steps, shift, points):
    steps = row_steps * column_steps + shift
    steps = steps - jnp.floor(steps * (1.0 / points)) * points
    return steps * (2.0 * jnp.pi / points)


def to_latitudes(
    levels,
    state_hbm,
    legendre_hbm,
    out_ref,
    fourier_ref,
    legendre_ref,
    state_ref,
    rows_ref,
    state_sems,
    legendre_sems,
):
    waves, rows, _ = state_hbm.shape
    copies = routes(waves, (state_hbm, state_ref, state_sems), (legendre_hbm, legendre_ref, legendre_sems))
    table_rows, points = fourier_ref.shape
    total = table_rows // 2
    row = lax.broadcasted_iota(jnp.int32, (table_rows, LANES), 0)
    lane = lax.broadcasted_iota(jnp.int32, (table_rows, LANES), 1).astype(jnp.float32)
    quarter = jnp.where(row >= total, points // 4, 0).astype(jnp.float32)
    order = jnp.where(row >= total, row - total, row).astype(jnp.float32)
    coarse = turns(order, lane * LANES, quarter, points)
    fine = turns(order[:total], lane[:total], 0.0, points)
    cos_coarse, sin_coarse = jnp.cos(coarse), jnp.sin(coarse)
    cos_fine, sin_fine = jnp.cos(fine), jnp.sin(fine)
    tiles = points // LANES
    for wave in range(waves):
        arrive(copies, wave)
        product = jnp.dot(
            state_ref[wave].astype(jnp.bfloat16),
            legendre_ref[wave],
            preferred_element_type=jnp.float32,
        )
        put_rows(rows_ref, 0, pl.ds(wave * rows, rows), product)
        for tile in range(wave * tiles // waves, (wave + 1) * tiles // waves):
            for part in range(2):
                here = slice(part * total, (part + 1) * total)
                fourier_ref[here, tile * LANES : (tile + 1) * LANES] = (
                    cos_coarse[here, tile : tile + 1] * cos_fine
                    - sin_coarse[here, tile : tile + 1] * sin_fine
                ).astype(jnp.bfloat16)
    width = out_ref.shape[2] // 2
    half = width // 2
    span = width // LANES
    left = lax.broadcasted_iota(jnp.int32, (waves, width), 1) < half
    for level in range(levels):
        for part in range(2):
            first = 2 * levels * part + level
            wind = get_rows(rows_ref, 0, span, pl.ds(first, waves, stride=rows))
            temper = get_rows(rows_ref, 0, span, pl.ds(first + levels, waves, stride=rows))
            low = jnp.where(left, wind, pltpu.roll(temper, half, 1))
            high = jnp.where(left, pltpu.roll(wind, half, 1), temper)
            here = slice(part * width, (part + 1) * width)
            out_ref[2 * level, :, here] = low.astype(jnp.bfloat16)
            out_ref[2 * level + 1, :, here] = high.astype(jnp.bfloat16)


def on_grid(
    synthesis_scale,
    analysis_scale,
    levels,
    region_smem,
    coef_ref,
    fourier_ref,
    lat_weights_ref,
    out_ref,
    weights_ref,
    turned_ref,
    total_ref,
    region_ref,
):
    points = fourier_ref.shape[1]
    every = lat_weights_ref.shape[0]
    lats = every // 2
    waves = coef_ref.shape[0]
    position = lax.axis_index("wave")
    lat_start = pl.multiple_of((position % 2) * lats, 8)
    weights_ref[...] = jnp.broadcast_to(lat_weights_ref[...].reshape(1, every), (8, every)).T
    weights = weights_ref[pl.ds(lat_start, lats), 0:1]
    for part in range(2):
        turned_ref[:, part * waves : (part + 1) * waves] = coef_ref[:, part * every : (part + 1) * every].T
    total_ref[...] = jnp.zeros_like(total_ref)
    region_ref[...] = jnp.zeros_like(region_ref)
    for part in range(points // COLUMNS):
        table = fourier_ref[:, part * COLUMNS : (part + 1) * COLUMNS]
        grid = synthesis_scale * jnp.dot(
            turned_ref[...], table, preferred_element_type=jnp.float32
        )
        wind, temper = grid[:lats], grid[lats:]
        weighted = wind * weights
        total_ref[:lats] += lax.dot_general(
            (0.5 * wind * weighted).astype(jnp.bfloat16),
            table,
            (((1,), (1,)), ((), ())),
            preferred_element_type=jnp.float32,
        )
        total_ref[lats:] += lax.dot_general(
            (weighted * temper).astype(jnp.bfloat16),
            table,
            (((1,), (1,)), ((), ())),
            preferred_element_type=jnp.float32,
        )
        column = part * COLUMNS + lax.broadcasted_iota(jnp.int32, (1, COLUMNS), 1)
        inside = (column >= region_smem[2]) & (column < region_smem[3])
        region_ref[...] += jnp.where(inside, temper * temper, 0.0)
    lat = lat_start + lax.broadcasted_iota(jnp.int32, (lats, 1), 0)
    lowest = position // 2 == levels - 1
    lat_inside = (lat >= region_smem[0]) & (lat < region_smem[1]) & lowest
    score = jnp.sum(
        jnp.where(lat_inside, weights, 0.0) * jnp.sum(region_ref[...], axis=1, keepdims=True),
        axis=0,
        keepdims=True,
    )
    score = jnp.broadcast_to(score, (waves, LANES))
    high = score.astype(jnp.bfloat16).astype(jnp.float32)
    middle = (score - high).astype(jnp.bfloat16).astype(jnp.float32)
    low = score - high - middle
    lane = lax.broadcasted_iota(jnp.int32, score.shape, 1)
    parts = jnp.where(lane == 0, high, jnp.where(lane == 1, middle, jnp.where(lane == 2, low, 0.0)))
    out_ref[:, 2 * every :] = parts.astype(jnp.bfloat16)
    for part in range(2):
        out_ref[:, part * every : (part + 1) * every] = (
            (analysis_scale * total_ref[:, part * waves : (part + 1) * waves]).T.astype(jnp.bfloat16)
        )


def to_degrees(
    levels,
    waves_total,
    region_smem,
    coef_ref,
    legendre_ref,
    state_ref,
    lat_weights_ref,
    out_ref,
    scores_ref,
    wide_ref,
):
    waves, degrees, lats = legendre_ref.shape
    owners = coef_ref.shape[0]
    half = lats // 2
    span = lats // LANES
    parts = jnp.zeros((1, LANES), jnp.float32)
    for owner in range(owners):
        values = coef_ref[owner].astype(jnp.float32)
        put_rows(wide_ref, 0, pl.ds(owner * waves, waves), values[:, : 2 * lats])
        parts += values[0:1, 2 * lats :]
    lat = lax.broadcasted_iota(jnp.int32, (1, lats), 1)
    inside = (lat >= region_smem[0]) & (lat < region_smem[1])
    weight = jnp.sum(jnp.where(inside, lat_weights_ref[...].reshape(1, lats), 0.0), axis=1, keepdims=True)
    columns = (region_smem[3] - region_smem[2]).astype(jnp.float32)
    scores_ref[...] = jnp.sum(parts, axis=1, keepdims=True) / (weight * columns)

    position = lax.axis_index("wave")
    degree = lax.broadcasted_iota(jnp.int32, (1, degrees), 1).astype(jnp.float32)
    damping = 1.0 + ((degree + 1.0) / degrees) ** 2
    left = lax.broadcasted_iota(jnp.int32, (levels, lats), 1) < half
    middle = 2 * levels
    for wave in range(waves):
        rows = []
        for part in range(2):
            first = get_rows(wide_ref, part * span, span, pl.ds(wave, levels, stride=2 * waves))
            second = get_rows(wide_ref, part * span, span, pl.ds(waves + wave, levels, stride=2 * waves))
            rows.append(jnp.where(left, first, pltpu.roll(second, half, 1)))
            rows.append(jnp.where(left, pltpu.roll(first, half, 1), second))
        tendency = lax.dot_general(
            jnp.concatenate(rows, axis=0).astype(jnp.bfloat16),
            legendre_ref[wave],
            (((1,), (1,)), ((), ())),
            preferred_element_type=jnp.float32,
        )
        global_wave = (position * waves + wave).astype(jnp.float32)
        advection = advect_rate * global_wave / waves_total
        out_ref[wave, :middle] = (
            (state_ref[wave, :middle] + advection * tendency[middle:]) / damping
        ).astype(jnp.bfloat16)
        out_ref[wave, middle:] = (
            (state_ref[wave, middle:] - advection * tendency[:middle]) / damping
        ).astype(jnp.bfloat16)


def pick(sources_smem, pieces_ref, out_ref):
    for slot in range(out_ref.shape[0]):
        out_ref[slot] = pieces_ref[sources_smem[slot]]


def on_device(state, legendre, lat_weights, region, sources):
    wave_count = lax.axis_size("wave")
    member_count = lax.axis_size("member")
    waves_local, degrees, latitudes = legendre.shape
    waves_total = waves_local * wave_count
    state_rows = state.shape[2]
    levels = state_rows // 4
    half = latitudes // 2
    spectral = state[0]
    lat_row = lat_weights
    whole = pl.BlockSpec(memory_space=pltpu.VMEM)
    scalars = pl.BlockSpec(memory_space=pltpu.SMEM)
    stay = pl.BlockSpec(memory_space=pltpu.HBM)
    small = pltpu.CompilerParams(vmem_limit_bytes=24 << 20)
    near = [
        pltpu.VMEM(legendre.shape, jnp.bfloat16),
        pltpu.VMEM(spectral.shape, jnp.float32),
    ]
    arrivals = [pltpu.SemaphoreType.DMA((waves_local,)), pltpu.SemaphoreType.DMA((waves_local,))]

    coef, fourier = pl.pallas_call(
        functools.partial(to_latitudes, levels),
        in_specs=[stay, stay],
        out_specs=[whole, whole],
        out_shape=[
            jax.ShapeDtypeStruct((wave_count, waves_local, 2 * latitudes), jnp.bfloat16),
            pltpu.VMEM((2 * waves_total, NLON), jnp.bfloat16),
        ],
        scratch_shapes=[
            *near,
            pltpu.VMEM((latitudes // LANES, waves_local * state_rows, LANES), jnp.float32),
            *arrivals,
        ],
        compiler_params=pltpu.CompilerParams(vmem_limit_bytes=52 << 20),
        name="to_latitudes",
    )(spectral, legendre)
    coef = lax.all_to_all(coef, "wave", split_axis=0, concat_axis=0, tiled=True)

    width = 2 * latitudes + LANES
    flux_coef = pl.pallas_call(
        functools.partial(on_grid, (2.0 * waves_total) ** (-0.5), NLON ** (-0.5), levels),
        in_specs=[scalars, whole, whole, whole],
        out_specs=whole,
        out_shape=jax.ShapeDtypeStruct((waves_total, width), jnp.bfloat16),
        scratch_shapes=[
            pltpu.VMEM((latitudes, 8), jnp.float32),
            pltpu.VMEM((latitudes, 2 * waves_total), jnp.bfloat16),
            pltpu.VMEM((latitudes, 2 * waves_total), jnp.float32),
            pltpu.VMEM((half, COLUMNS), jnp.float32),
        ],
        compiler_params=small,
        name="on_grid",
    )(region, coef.reshape(waves_total, 2 * latitudes), fourier, lat_row)
    flux_coef = lax.all_to_all(
        flux_coef.reshape(wave_count, waves_local, width), "wave", split_axis=0, concat_axis=0, tiled=True
    )

    stepped, scores = pl.pallas_call(
        functools.partial(to_degrees, levels, waves_total),
        in_specs=[scalars, whole, whole, whole, whole],
        out_specs=[whole, whole],
        out_shape=[
            jax.ShapeDtypeStruct((waves_local, state_rows, degrees), jnp.bfloat16),
            jax.ShapeDtypeStruct((1, 1), jnp.float32),
        ],
        scratch_shapes=[
            pltpu.VMEM((2 * latitudes // LANES, wave_count * waves_local, LANES), jnp.float32)
        ],
        compiler_params=small,
        name="to_degrees",
    )(region, flux_coef, legendre, spectral, lat_row)

    piece_rows = waves_local * state_rows // member_count
    pieces = lax.all_to_all(
        stepped.reshape(member_count, piece_rows, degrees),
        "member",
        split_axis=0,
        concat_axis=0,
        tiled=True,
    )
    picked = pl.pallas_call(
        pick,
        in_specs=[scalars, whole],
        out_specs=whole,
        out_shape=jax.ShapeDtypeStruct(pieces.shape, jnp.bfloat16),
        compiler_params=small,
        name="pick",
    )(sources, pieces)
    cloned = lax.all_to_all(picked, "member", split_axis=0, concat_axis=0, tiled=True)
    cloned = cloned.reshape(1, waves_local, state_rows, degrees).astype(jnp.float32)
    return (cloned, scores.reshape(1))


def solution(mesh):
    in_specs = (P("member", "wave", None, None), P("wave", None, None), P(), P(), P())
    out_specs = (P("member", "wave", None, None), P("member"))
    return jax.shard_map(
        on_device, mesh=mesh, in_specs=in_specs, out_specs=out_specs, check_vma=False
    )
```

```python
import functools

import jax
import jax.numpy as jnp
from jax import lax
from jax.experimental import pallas as pl
from jax.experimental.pallas import tpu as pltpu
from jax.sharding import PartitionSpec as P

NLON = 2560
LANES = 128
COLUMNS = 256
AHEAD = 8

advect_rate = 2.0


def put_rows(tiles_ref, first_tile, where, values):
    for tile in range(values.shape[1] // LANES):
        tiles_ref[first_tile + tile, where, :] = values[:, tile * LANES : (tile + 1) * LANES]


def get_rows(tiles_ref, first_tile, tiles, where):
    return jnp.concatenate([tiles_ref[first_tile + tile, where, :] for tile in range(tiles)], axis=1)


def routes(waves, *pairs):
    copies = [
        [pltpu.make_async_copy(far.at[wave], near.at[wave], sems.at[wave]) for far, near, sems in pairs]
        for wave in range(waves)
    ]
    for group in copies[:AHEAD]:
        for copy in group:
            copy.start()
    return copies


def arrive(copies, wave):
    for copy in copies[wave]:
        copy.wait()
    for copy in copies[wave + AHEAD] if wave + AHEAD < len(copies) else ():
        copy.start()


def turns(row_steps, column_steps, shift, points):
    steps = row_steps * column_steps + shift
    steps = steps - jnp.floor(steps * (1.0 / points)) * points
    return steps * (2.0 * jnp.pi / points)


def to_latitudes(
    levels,
    state_hbm,
    legendre_hbm,
    out_ref,
    fourier_ref,
    legendre_ref,
    state_ref,
    rows_ref,
    state_sems,
    legendre_sems,
):
    waves, rows, _ = state_hbm.shape
    copies = routes(waves, (state_hbm, state_ref, state_sems), (legendre_hbm, legendre_ref, legendre_sems))
    table_rows, points = fourier_ref.shape
    total = table_rows // 2
    row = lax.broadcasted_iota(jnp.int32, (table_rows, LANES), 0)
    lane = lax.broadcasted_iota(jnp.int32, (table_rows, LANES), 1).astype(jnp.float32)
    quarter = jnp.where(row >= total, points // 4, 0).astype(jnp.float32)
    order = jnp.where(row >= total, row - total, row).astype(jnp.float32)
    coarse = turns(order, lane * LANES, quarter, points)
    fine = turns(order[:total], lane[:total], 0.0, points)
    cos_coarse, sin_coarse = jnp.cos(coarse), jnp.sin(coarse)
    cos_fine, sin_fine = jnp.cos(fine), jnp.sin(fine)
    tiles = points // LANES
    for wave in range(waves):
        arrive(copies, wave)
        product = jnp.dot(
            state_ref[wave].astype(jnp.bfloat16),
            legendre_ref[wave],
            preferred_element_type=jnp.float32,
        )
        put_rows(rows_ref, 0, pl.ds(wave * rows, rows), product)
        for tile in range(wave * tiles // waves, (wave + 1) * tiles // waves):
            for part in range(2):
                here = slice(part * total, (part + 1) * total)
                fourier_ref[here, tile * LANES : (tile + 1) * LANES] = (
                    cos_coarse[here, tile : tile + 1] * cos_fine
                    - sin_coarse[here, tile : tile + 1] * sin_fine
                ).astype(jnp.bfloat16)
    width = out_ref.shape[2] // 2
    half = width // 2
    span = width // LANES
    left = lax.broadcasted_iota(jnp.int32, (waves, width), 1) < half
    for level in range(levels):
        for part in range(2):
            first = 2 * levels * part + level
            wind = get_rows(rows_ref, 0, span, pl.ds(first, waves, stride=rows))
            temper = get_rows(rows_ref, 0, span, pl.ds(first + levels, waves, stride=rows))
            low = jnp.where(left, wind, pltpu.roll(temper, half, 1))
            high = jnp.where(left, pltpu.roll(wind, half, 1), temper)
            here = slice(part * width, (part + 1) * width)
            out_ref[2 * level, :, here] = low.astype(jnp.bfloat16)
            out_ref[2 * level + 1, :, here] = high.astype(jnp.bfloat16)


def on_grid(
    synthesis_scale,
    analysis_scale,
    levels,
    region_smem,
    coef_ref,
    fourier_ref,
    lat_weights_ref,
    out_ref,
    weights_ref,
    turned_ref,
    total_ref,
):
    points = fourier_ref.shape[1]
    every = lat_weights_ref.shape[0]
    lats = every // 2
    waves = coef_ref.shape[0]
    position = lax.axis_index("wave")
    lat_start = pl.multiple_of((position % 2) * lats, 8)
    weights_ref[...] = jnp.broadcast_to(lat_weights_ref[...].reshape(1, every), (8, every)).T
    weights = weights_ref[pl.ds(lat_start, lats), 0:1] * (synthesis_scale * synthesis_scale)
    for part in range(2):
        turned_ref[:, part * waves : (part + 1) * waves] = coef_ref[:, part * every : (part + 1) * every].T
    region_sum = jnp.zeros((lats, LANES), jnp.float32)
    for part in range(points // COLUMNS):
        table = fourier_ref[:, part * COLUMNS : (part + 1) * COLUMNS]
        grid = jnp.dot(turned_ref[...], table, preferred_element_type=jnp.float32)
        wind, temper = grid[:lats], grid[lats:]
        weighted = wind * weights
        for rows, flux in ((slice(0, lats), wind * weighted), (slice(lats, every), weighted * temper)):
            term = lax.dot_general(
                flux.astype(jnp.bfloat16),
                table,
                (((1,), (1,)), ((), ())),
                preferred_element_type=jnp.float32,
            )
            total_ref[rows] = term if part == 0 else total_ref[rows] + term
        column = part * COLUMNS + lax.broadcasted_iota(jnp.int32, (1, COLUMNS), 1)
        inside = (column >= region_smem[2]) & (column < region_smem[3])
        squares = jnp.where(inside, temper * temper, 0.0)
        for tile in range(COLUMNS // LANES):
            region_sum += squares[:, tile * LANES : (tile + 1) * LANES]
    lat = lat_start + lax.broadcasted_iota(jnp.int32, (lats, 1), 0)
    lowest = position // 2 == levels - 1
    lat_inside = (lat >= region_smem[0]) & (lat < region_smem[1]) & lowest
    score = jnp.sum(
        jnp.where(lat_inside, weights, 0.0) * jnp.sum(region_sum, axis=1, keepdims=True),
        axis=0,
        keepdims=True,
    )
    score = jnp.broadcast_to(score, (waves, LANES))
    high = score.astype(jnp.bfloat16).astype(jnp.float32)
    middle = (score - high).astype(jnp.bfloat16).astype(jnp.float32)
    low = score - high - middle
    lane = lax.broadcasted_iota(jnp.int32, score.shape, 1)
    parts = jnp.where(lane == 0, high, jnp.where(lane == 1, middle, jnp.where(lane == 2, low, 0.0)))
    out_ref[:, 2 * every :] = parts.astype(jnp.bfloat16)
    row = lax.broadcasted_iota(jnp.int32, (every, 1), 0)
    scale = jnp.where(row < lats, 0.5 * analysis_scale, analysis_scale)
    for part in range(2):
        out_ref[:, part * every : (part + 1) * every] = (
            (scale * total_ref[:, part * waves : (part + 1) * waves]).astype(jnp.bfloat16).T
        )


def to_degrees(
    levels,
    waves_total,
    region_smem,
    coef_ref,
    legendre_ref,
    state_ref,
    lat_weights_ref,
    out_ref,
    scores_ref,
    wide_ref,
):
    waves, degrees, lats = legendre_ref.shape
    owners = coef_ref.shape[0]
    half = lats // 2
    span = lats // LANES
    parts = jnp.zeros((1, LANES), jnp.float32)
    for owner in range(owners):
        values = coef_ref[owner].astype(jnp.float32)
        put_rows(wide_ref, 0, pl.ds(owner * waves, waves), values[:, : 2 * lats])
        parts += values[0:1, 2 * lats :]
    lat = lax.broadcasted_iota(jnp.int32, (1, lats), 1)
    inside = (lat >= region_smem[0]) & (lat < region_smem[1])
    weight = jnp.sum(jnp.where(inside, lat_weights_ref[...].reshape(1, lats), 0.0), axis=1, keepdims=True)
    columns = (region_smem[3] - region_smem[2]).astype(jnp.float32)
    scores_ref[...] = jnp.sum(parts, axis=1, keepdims=True) / (weight * columns)

    position = lax.axis_index("wave")
    degree = lax.broadcasted_iota(jnp.int32, (1, degrees), 1).astype(jnp.float32)
    undamped = 1.0 / (1.0 + ((degree + 1.0) / degrees) ** 2)
    left = lax.broadcasted_iota(jnp.int32, (levels, lats), 1) < half
    middle = 2 * levels
    for wave in range(waves):
        rows = []
        for part in range(2):
            first = get_rows(wide_ref, part * span, span, pl.ds(wave, levels, stride=2 * waves))
            second = get_rows(wide_ref, part * span, span, pl.ds(waves + wave, levels, stride=2 * waves))
            rows.append(jnp.where(left, first, pltpu.roll(second, half, 1)))
            rows.append(jnp.where(left, pltpu.roll(first, half, 1), second))
        tendency = lax.dot_general(
            jnp.concatenate(rows, axis=0).astype(jnp.bfloat16),
            legendre_ref[wave],
            (((1,), (1,)), ((), ())),
            preferred_element_type=jnp.float32,
        )
        global_wave = (position * waves + wave).astype(jnp.float32)
        advection = advect_rate * global_wave / waves_total
        out_ref[wave, :middle] = (
            (state_ref[wave, :middle] + advection * tendency[middle:]) * undamped
        ).astype(jnp.bfloat16)
        out_ref[wave, middle:] = (
            (state_ref[wave, middle:] - advection * tendency[:middle]) * undamped
        ).astype(jnp.bfloat16)


def pick(sources_smem, pieces_ref, out_ref):
    for slot in range(out_ref.shape[0]):
        out_ref[slot] = pieces_ref[sources_smem[slot]]


def on_device(state, legendre, lat_weights, region, sources):
    wave_count = lax.axis_size("wave")
    member_count = lax.axis_size("member")
    waves_local, degrees, latitudes = legendre.shape
    waves_total = waves_local * wave_count
    state_rows = state.shape[2]
    levels = state_rows // 4
    spectral = state[0]
    lat_row = lat_weights
    whole = pl.BlockSpec(memory_space=pltpu.VMEM)
    scalars = pl.BlockSpec(memory_space=pltpu.SMEM)
    stay = pl.BlockSpec(memory_space=pltpu.HBM)
    small = pltpu.CompilerParams(vmem_limit_bytes=16 << 20)
    near = [
        pltpu.VMEM(legendre.shape, jnp.bfloat16),
        pltpu.VMEM(spectral.shape, jnp.float32),
    ]
    arrivals = [pltpu.SemaphoreType.DMA((waves_local,)), pltpu.SemaphoreType.DMA((waves_local,))]

    coef, fourier, legendre_near = pl.pallas_call(
        functools.partial(to_latitudes, levels),
        in_specs=[stay, stay],
        out_specs=[whole, whole, whole],
        out_shape=[
            pltpu.VMEM((wave_count, waves_local, 2 * latitudes), jnp.bfloat16),
            pltpu.VMEM((2 * waves_total, NLON), jnp.bfloat16),
            pltpu.VMEM(legendre.shape, jnp.bfloat16),
        ],
        scratch_shapes=[
            pltpu.VMEM(spectral.shape, jnp.float32),
            pltpu.VMEM((latitudes // LANES, waves_local * state_rows, LANES), jnp.float32),
            *arrivals,
        ],
        compiler_params=pltpu.CompilerParams(vmem_limit_bytes=52 << 20),
        name="to_latitudes",
    )(spectral, legendre)
    coef = lax.all_to_all(coef, "wave", split_axis=0, concat_axis=0, tiled=True)

    width = 2 * latitudes + LANES
    flux_coef = pl.pallas_call(
        functools.partial(on_grid, (2.0 * waves_total) ** (-0.5), NLON ** (-0.5), levels),
        in_specs=[scalars, whole, whole, whole],
        out_specs=whole,
        out_shape=jax.ShapeDtypeStruct((waves_total, width), jnp.bfloat16),
        scratch_shapes=[
            pltpu.VMEM((latitudes, 8), jnp.float32),
            pltpu.VMEM((latitudes, 2 * waves_total), jnp.bfloat16),
            pltpu.VMEM((latitudes, 2 * waves_total), jnp.float32),
        ],
        compiler_params=small,
        name="on_grid",
    )(region, coef.reshape(waves_total, 2 * latitudes), fourier, lat_row)
    flux_coef = lax.all_to_all(
        flux_coef.reshape(wave_count, waves_local, width), "wave", split_axis=0, concat_axis=0, tiled=True
    )

    stepped, scores = pl.pallas_call(
        functools.partial(to_degrees, levels, waves_total),
        in_specs=[scalars, whole, whole, whole, whole],
        out_specs=[whole, whole],
        out_shape=[
            jax.ShapeDtypeStruct((waves_local, state_rows, degrees), jnp.bfloat16),
            jax.ShapeDtypeStruct((1, 1), jnp.float32),
        ],
        scratch_shapes=[
            pltpu.VMEM((2 * latitudes // LANES, wave_count * waves_local, LANES), jnp.float32)
        ],
        compiler_params=small,
        name="to_degrees",
    )(region, flux_coef, legendre_near, spectral, lat_row)

    piece_rows = waves_local * state_rows // member_count
    pieces = lax.all_to_all(
        stepped.reshape(member_count, piece_rows, degrees),
        "member",
        split_axis=0,
        concat_axis=0,
        tiled=True,
    )
    picked = pl.pallas_call(
        pick,
        in_specs=[scalars, whole],
        out_specs=whole,
        out_shape=jax.ShapeDtypeStruct(pieces.shape, jnp.bfloat16),
        compiler_params=small,
        name="pick",
    )(sources, pieces)
    cloned = lax.all_to_all(picked, "member", split_axis=0, concat_axis=0, tiled=True)
    cloned = cloned.reshape(1, waves_local, state_rows, degrees).astype(jnp.float32)
    return (cloned, scores.reshape(1))


def solution(mesh):
    in_specs = (P("member", "wave", None, None), P("wave", None, None), P(), P(), P())
    out_specs = (P("member", "wave", None, None), P("member"))
    return jax.shard_map(
        on_device, mesh=mesh, in_specs=in_specs, out_specs=out_specs, check_vma=False
    )
```

```python
import functools

import jax
import jax.numpy as jnp
from jax import lax
from jax.experimental import pallas as pl
from jax.experimental.pallas import tpu as pltpu
from jax.sharding import PartitionSpec as P

NLON = 2560
LANES = 128
COLUMNS = 256
AHEAD = 8

advect_rate = 2.0


def put_rows(tiles_ref, first_tile, where, values):
    for tile in range(values.shape[1] // LANES):
        tiles_ref[first_tile + tile, where, :] = values[:, tile * LANES : (tile + 1) * LANES]


def get_rows(tiles_ref, first_tile, tiles, where):
    return jnp.concatenate([tiles_ref[first_tile + tile, where, :] for tile in range(tiles)], axis=1)


def routes(waves, *pairs):
    copies = [
        [pltpu.make_async_copy(far.at[wave], near.at[wave], sems.at[wave]) for far, near, sems in pairs]
        for wave in range(waves)
    ]
    for group in copies[:AHEAD]:
        for copy in group:
            copy.start()
    return copies


def arrive(copies, wave):
    for copy in copies[wave]:
        copy.wait()
    for copy in copies[wave + AHEAD] if wave + AHEAD < len(copies) else ():
        copy.start()


def turns(row_steps, column_steps, shift, points):
    steps = row_steps * column_steps + shift
    steps = steps - jnp.floor(steps * (1.0 / points)) * points
    return steps * (2.0 * jnp.pi / points)


def to_latitudes(
    levels,
    state_hbm,
    legendre_hbm,
    out_ref,
    fourier_ref,
    legendre_ref,
    state_ref,
    rows_ref,
    state_sems,
    legendre_sems,
):
    waves, rows, _ = state_hbm.shape
    copies = routes(waves, (state_hbm, state_ref, state_sems), (legendre_hbm, legendre_ref, legendre_sems))
    table_rows, points = fourier_ref.shape
    total = table_rows // 2
    row = lax.broadcasted_iota(jnp.int32, (table_rows, LANES), 0)
    lane = lax.broadcasted_iota(jnp.int32, (table_rows, LANES), 1).astype(jnp.float32)
    quarter = jnp.where(row >= total, points // 4, 0).astype(jnp.float32)
    order = jnp.where(row >= total, row - total, row).astype(jnp.float32)
    coarse = turns(order, lane * LANES, quarter, points)
    fine = turns(order[:total], lane[:total], 0.0, points)
    cos_coarse, sin_coarse = jnp.cos(coarse), jnp.sin(coarse)
    cos_fine, sin_fine = jnp.cos(fine), jnp.sin(fine)
    tiles = points // LANES
    for wave in range(waves):
        arrive(copies, wave)
        product = jnp.dot(
            state_ref[wave].astype(jnp.bfloat16),
            legendre_ref[wave],
            preferred_element_type=jnp.float32,
        )
        put_rows(rows_ref, 0, pl.ds(wave, rows, stride=waves), product)
        for tile in range(wave * tiles // waves, (wave + 1) * tiles // waves):
            for part in range(2):
                here = slice(part * total, (part + 1) * total)
                fourier_ref[here, tile * LANES : (tile + 1) * LANES] = (
                    cos_coarse[here, tile : tile + 1] * cos_fine
                    - sin_coarse[here, tile : tile + 1] * sin_fine
                ).astype(jnp.bfloat16)
    width = out_ref.shape[2] // 2
    half = width // 2
    span = width // LANES
    left = lax.broadcasted_iota(jnp.int32, (waves, width), 1) < half
    for level in range(levels):
        for part in range(2):
            first = 2 * levels * part + level
            wind = get_rows(rows_ref, 0, span, pl.ds(first * waves, waves))
            temper = get_rows(rows_ref, 0, span, pl.ds((first + levels) * waves, waves))
            low = jnp.where(left, wind, pltpu.roll(temper, half, 1))
            high = jnp.where(left, pltpu.roll(wind, half, 1), temper)
            here = slice(part * width, (part + 1) * width)
            out_ref[2 * level, :, here] = low.astype(jnp.bfloat16)
            out_ref[2 * level + 1, :, here] = high.astype(jnp.bfloat16)


def on_grid(
    synthesis_scale,
    analysis_scale,
    levels,
    region_smem,
    coef_ref,
    fourier_ref,
    lat_weights_ref,
    out_ref,
    weights_ref,
    turned_ref,
    total_ref,
):
    points = fourier_ref.shape[1]
    every = lat_weights_ref.shape[0]
    lats = every // 2
    waves = coef_ref.shape[0]
    position = lax.axis_index("wave")
    lat_start = pl.multiple_of((position % 2) * lats, 8)
    weights_ref[...] = jnp.broadcast_to(lat_weights_ref[...].reshape(1, every), (8, every)).T
    weights = weights_ref[pl.ds(lat_start, lats), 0:1] * (synthesis_scale * synthesis_scale)
    for part in range(2):
        turned_ref[:, part * waves : (part + 1) * waves] = coef_ref[:, part * every : (part + 1) * every].T
    region_sum = jnp.zeros((lats, LANES), jnp.float32)
    for part in range(points // COLUMNS):
        table = fourier_ref[:, part * COLUMNS : (part + 1) * COLUMNS]
        grid = jnp.dot(turned_ref[...], table, preferred_element_type=jnp.float32)
        wind, temper = grid[:lats], grid[lats:]
        weighted = wind * weights
        for rows, flux in ((slice(0, lats), wind * weighted), (slice(lats, every), weighted * temper)):
            term = lax.dot_general(
                flux.astype(jnp.bfloat16),
                table,
                (((1,), (1,)), ((), ())),
                preferred_element_type=jnp.float32,
            )
            total_ref[rows] = term if part == 0 else total_ref[rows] + term
        column = part * COLUMNS + lax.broadcasted_iota(jnp.int32, (1, COLUMNS), 1)
        inside = (column >= region_smem[2]) & (column < region_smem[3])
        squares = jnp.where(inside, temper * temper, 0.0)
        for tile in range(COLUMNS // LANES):
            region_sum += squares[:, tile * LANES : (tile + 1) * LANES]
    lat = lat_start + lax.broadcasted_iota(jnp.int32, (lats, 1), 0)
    lowest = position // 2 == levels - 1
    lat_inside = (lat >= region_smem[0]) & (lat < region_smem[1]) & lowest
    score = jnp.sum(
        jnp.where(lat_inside, weights, 0.0) * jnp.sum(region_sum, axis=1, keepdims=True),
        axis=0,
        keepdims=True,
    )
    score = jnp.broadcast_to(score, (waves, LANES))
    high = score.astype(jnp.bfloat16).astype(jnp.float32)
    middle = (score - high).astype(jnp.bfloat16).astype(jnp.float32)
    low = score - high - middle
    lane = lax.broadcasted_iota(jnp.int32, score.shape, 1)
    parts = jnp.where(lane == 0, high, jnp.where(lane == 1, middle, jnp.where(lane == 2, low, 0.0)))
    out_ref[:, 2 * every :] = parts.astype(jnp.bfloat16)
    row = lax.broadcasted_iota(jnp.int32, (every, 1), 0)
    scale = jnp.where(row < lats, 0.5 * analysis_scale, analysis_scale)
    for part in range(2):
        out_ref[:, part * every : (part + 1) * every] = (
            (scale * total_ref[:, part * waves : (part + 1) * waves]).astype(jnp.bfloat16).T
        )


def to_degrees(
    levels,
    waves_total,
    region_smem,
    coef_ref,
    legendre_ref,
    state_ref,
    lat_weights_ref,
    out_ref,
    scores_ref,
    wide_ref,
):
    waves, degrees, lats = legendre_ref.shape
    owners = coef_ref.shape[0]
    half = lats // 2
    span = lats // LANES
    parts = jnp.zeros((1, LANES), jnp.float32)
    for owner in range(owners):
        values = coef_ref[owner].astype(jnp.float32)
        put_rows(wide_ref, 0, pl.ds(owner * waves, waves), values[:, : 2 * lats])
        parts += values[0:1, 2 * lats :]
    lat = lax.broadcasted_iota(jnp.int32, (1, lats), 1)
    inside = (lat >= region_smem[0]) & (lat < region_smem[1])
    weight = jnp.sum(jnp.where(inside, lat_weights_ref[...].reshape(1, lats), 0.0), axis=1, keepdims=True)
    columns = (region_smem[3] - region_smem[2]).astype(jnp.float32)
    scores_ref[...] = jnp.sum(parts, axis=1, keepdims=True) / (weight * columns)

    position = lax.axis_index("wave")
    degree = lax.broadcasted_iota(jnp.int32, (1, degrees), 1).astype(jnp.float32)
    undamped = 1.0 / (1.0 + ((degree + 1.0) / degrees) ** 2)
    left = lax.broadcasted_iota(jnp.int32, (levels, lats), 1) < half
    middle = 2 * levels
    for wave in range(waves):
        rows = []
        for part in range(2):
            first = get_rows(wide_ref, part * span, span, pl.ds(wave, levels, stride=2 * waves))
            second = get_rows(wide_ref, part * span, span, pl.ds(waves + wave, levels, stride=2 * waves))
            rows.append(jnp.where(left, first, pltpu.roll(second, half, 1)))
            rows.append(jnp.where(left, pltpu.roll(first, half, 1), second))
        tendency = lax.dot_general(
            legendre_ref[wave],
            jnp.concatenate(rows, axis=0).astype(jnp.bfloat16),
            (((1,), (1,)), ((), ())),
            preferred_element_type=jnp.float32,
        ).T
        global_wave = (position * waves + wave).astype(jnp.float32)
        advection = advect_rate * global_wave / waves_total
        out_ref[wave, :middle] = (
            (state_ref[wave, :middle] + advection * tendency[middle:]) * undamped
        ).astype(jnp.bfloat16)
        out_ref[wave, middle:] = (
            (state_ref[wave, middle:] - advection * tendency[:middle]) * undamped
        ).astype(jnp.bfloat16)


def pick(sources_smem, pieces_ref, out_ref):
    for slot in range(out_ref.shape[0]):
        out_ref[slot] = pieces_ref[sources_smem[slot]]


def on_device(state, legendre, lat_weights, region, sources):
    wave_count = lax.axis_size("wave")
    member_count = lax.axis_size("member")
    waves_local, degrees, latitudes = legendre.shape
    waves_total = waves_local * wave_count
    state_rows = state.shape[2]
    levels = state_rows // 4
    spectral = state[0]
    lat_row = lat_weights
    whole = pl.BlockSpec(memory_space=pltpu.VMEM)
    scalars = pl.BlockSpec(memory_space=pltpu.SMEM)
    stay = pl.BlockSpec(memory_space=pltpu.HBM)
    small = pltpu.CompilerParams(vmem_limit_bytes=16 << 20)
    near = [
        pltpu.VMEM(legendre.shape, jnp.bfloat16),
        pltpu.VMEM(spectral.shape, jnp.float32),
    ]
    arrivals = [pltpu.SemaphoreType.DMA((waves_local,)), pltpu.SemaphoreType.DMA((waves_local,))]

    coef, fourier, legendre_near = pl.pallas_call(
        functools.partial(to_latitudes, levels),
        in_specs=[stay, stay],
        out_specs=[whole, whole, whole],
        out_shape=[
            pltpu.VMEM((wave_count, waves_local, 2 * latitudes), jnp.bfloat16),
            pltpu.VMEM((2 * waves_total, NLON), jnp.bfloat16),
            pltpu.VMEM(legendre.shape, jnp.bfloat16),
        ],
        scratch_shapes=[
            pltpu.VMEM(spectral.shape, jnp.float32),
            pltpu.VMEM((latitudes // LANES, waves_local * state_rows, LANES), jnp.float32),
            *arrivals,
        ],
        compiler_params=pltpu.CompilerParams(vmem_limit_bytes=52 << 20),
        name="to_latitudes",
    )(spectral, legendre)
    coef = lax.all_to_all(coef, "wave", split_axis=0, concat_axis=0, tiled=True)

    width = 2 * latitudes + LANES
    flux_coef = pl.pallas_call(
        functools.partial(on_grid, (2.0 * waves_total) ** (-0.5), NLON ** (-0.5), levels),
        in_specs=[scalars, whole, whole, whole],
        out_specs=whole,
        out_shape=jax.ShapeDtypeStruct((waves_total, width), jnp.bfloat16),
        scratch_shapes=[
            pltpu.VMEM((latitudes, 8), jnp.float32),
            pltpu.VMEM((latitudes, 2 * waves_total), jnp.bfloat16),
            pltpu.VMEM((latitudes, 2 * waves_total), jnp.float32),
        ],
        compiler_params=small,
        name="on_grid",
    )(region, coef.reshape(waves_total, 2 * latitudes), fourier, lat_row)
    flux_coef = lax.all_to_all(
        flux_coef.reshape(wave_count, waves_local, width), "wave", split_axis=0, concat_axis=0, tiled=True
    )

    stepped, scores = pl.pallas_call(
        functools.partial(to_degrees, levels, waves_total),
        in_specs=[scalars, whole, whole, whole, whole],
        out_specs=[whole, whole],
        out_shape=[
            jax.ShapeDtypeStruct((waves_local, state_rows, degrees), jnp.bfloat16),
            jax.ShapeDtypeStruct((1, 1), jnp.float32),
        ],
        scratch_shapes=[
            pltpu.VMEM((2 * latitudes // LANES, wave_count * waves_local, LANES), jnp.float32)
        ],
        compiler_params=small,
        name="to_degrees",
    )(region, flux_coef, legendre_near, spectral, lat_row)

    piece_rows = waves_local * state_rows // member_count
    pieces = lax.all_to_all(
        stepped.reshape(member_count, piece_rows, degrees),
        "member",
        split_axis=0,
        concat_axis=0,
        tiled=True,
    )
    picked = pl.pallas_call(
        pick,
        in_specs=[scalars, whole],
        out_specs=whole,
        out_shape=jax.ShapeDtypeStruct(pieces.shape, jnp.bfloat16),
        compiler_params=small,
        name="pick",
    )(sources, pieces)
    cloned = lax.all_to_all(picked, "member", split_axis=0, concat_axis=0, tiled=True)
    cloned = cloned.reshape(1, waves_local, state_rows, degrees).astype(jnp.float32)
    return (cloned, scores.reshape(1))


def solution(mesh):
    in_specs = (P("member", "wave", None, None), P("wave", None, None), P(), P(), P())
    out_specs = (P("member", "wave", None, None), P("member"))
    return jax.shard_map(
        on_device, mesh=mesh, in_specs=in_specs, out_specs=out_specs, check_vma=False
    )
```

```python
import functools

import jax
import jax.numpy as jnp
from jax import lax
from jax.experimental import pallas as pl
from jax.experimental.pallas import tpu as pltpu
from jax.sharding import PartitionSpec as P

NLON = 2560
LANES = 128
COLUMNS = 256
AHEAD = 8

advect_rate = 2.0


def put_rows(tiles_ref, first_tile, where, values):
    for tile in range(values.shape[1] // LANES):
        tiles_ref[first_tile + tile, where, :] = values[:, tile * LANES : (tile + 1) * LANES]


def get_rows(tiles_ref, first_tile, tiles, where):
    return jnp.concatenate([tiles_ref[first_tile + tile, where, :] for tile in range(tiles)], axis=1)


def routes(waves, *pairs):
    copies = [
        [pltpu.make_async_copy(far.at[wave], near.at[wave], sems.at[wave]) for far, near, sems in pairs]
        for wave in range(waves)
    ]
    for group in copies[:AHEAD]:
        for copy in group:
            copy.start()
    return copies


def arrive(copies, wave):
    for copy in copies[wave]:
        copy.wait()
    for copy in copies[wave + AHEAD] if wave + AHEAD < len(copies) else ():
        copy.start()


def turns(row_steps, column_steps, shift, points):
    steps = row_steps * column_steps + shift
    steps = steps - jnp.floor(steps * (1.0 / points)) * points
    return steps * (2.0 * jnp.pi / points)


def to_latitudes(
    levels,
    state_hbm,
    legendre_hbm,
    out_ref,
    fourier_ref,
    legendre_ref,
    state_ref,
    rows_ref,
    state_sems,
    legendre_sems,
):
    waves, rows, _ = state_hbm.shape
    copies = routes(waves, (state_hbm, state_ref, state_sems), (legendre_hbm, legendre_ref, legendre_sems))
    table_rows, points = fourier_ref.shape
    total = table_rows // 2
    row = lax.broadcasted_iota(jnp.int32, (table_rows, LANES), 0)
    lane = lax.broadcasted_iota(jnp.int32, (table_rows, LANES), 1).astype(jnp.float32)
    quarter = jnp.where(row >= total, points // 4, 0).astype(jnp.float32)
    order = jnp.where(row >= total, row - total, row).astype(jnp.float32)
    coarse = turns(order, lane * LANES, quarter, points)
    fine = turns(order[:total], lane[:total], 0.0, points)
    cos_coarse, sin_coarse = jnp.cos(coarse), jnp.sin(coarse)
    cos_fine, sin_fine = jnp.cos(fine), jnp.sin(fine)
    tiles = points // LANES
    for wave in range(waves):
        arrive(copies, wave)
        product = jnp.dot(
            state_ref[wave].astype(jnp.bfloat16),
            legendre_ref[wave],
            preferred_element_type=jnp.float32,
        )
        put_rows(rows_ref, 0, pl.ds(wave, rows, stride=waves), product)
        for tile in range(wave * tiles // waves, (wave + 1) * tiles // waves):
            for part in range(2):
                here = slice(part * total, (part + 1) * total)
                fourier_ref[here, tile * LANES : (tile + 1) * LANES] = (
                    cos_coarse[here, tile : tile + 1] * cos_fine
                    - sin_coarse[here, tile : tile + 1] * sin_fine
                ).astype(jnp.bfloat16)
    width = out_ref.shape[2] // 2
    half = width // 2
    span = width // LANES
    left = lax.broadcasted_iota(jnp.int32, (waves, width), 1) < half
    for level in range(levels):
        for part in range(2):
            first = 2 * levels * part + level
            wind = get_rows(rows_ref, 0, span, pl.ds(first * waves, waves))
            temper = get_rows(rows_ref, 0, span, pl.ds((first + levels) * waves, waves))
            low = jnp.where(left, wind, pltpu.roll(temper, half, 1))
            high = jnp.where(left, pltpu.roll(wind, half, 1), temper)
            here = slice(part * width, (part + 1) * width)
            out_ref[2 * level, :, here] = low.astype(jnp.bfloat16)
            out_ref[2 * level + 1, :, here] = high.astype(jnp.bfloat16)


def on_grid(
    synthesis_scale,
    analysis_scale,
    levels,
    region_smem,
    coef_ref,
    fourier_ref,
    lat_weights_ref,
    out_ref,
    weights_ref,
    turned_ref,
    total_ref,
):
    points = fourier_ref.shape[1]
    every = lat_weights_ref.shape[0]
    lats = every // 2
    waves = coef_ref.shape[0]
    position = lax.axis_index("wave")
    lat_start = pl.multiple_of((position % 2) * lats, 8)
    weights_ref[...] = jnp.broadcast_to(lat_weights_ref[...].reshape(1, every), (8, every)).T
    weights = weights_ref[pl.ds(lat_start, lats), 0:1] * (synthesis_scale * synthesis_scale)
    for part in range(2):
        turned_ref[:, part * waves : (part + 1) * waves] = coef_ref[:, part * every : (part + 1) * every].T
    region_sum = jnp.zeros((lats, LANES), jnp.float32)
    for part in range(points // COLUMNS):
        table = fourier_ref[:, part * COLUMNS : (part + 1) * COLUMNS]
        grid = jnp.dot(turned_ref[...], table, preferred_element_type=jnp.float32)
        wind, temper = grid[:lats], grid[lats:]
        weighted = wind * weights
        for rows, flux in ((slice(0, lats), wind * weighted), (slice(lats, every), weighted * temper)):
            term = lax.dot_general(
                flux.astype(jnp.bfloat16),
                table,
                (((1,), (1,)), ((), ())),
                preferred_element_type=jnp.float32,
            )
            total_ref[rows] = term if part == 0 else total_ref[rows] + term
        column = part * COLUMNS + lax.broadcasted_iota(jnp.int32, (1, COLUMNS), 1)
        inside = (column >= region_smem[2]) & (column < region_smem[3])
        squares = jnp.where(inside, temper * temper, 0.0)
        for tile in range(COLUMNS // LANES):
            region_sum += squares[:, tile * LANES : (tile + 1) * LANES]
    lat = lat_start + lax.broadcasted_iota(jnp.int32, (lats, 1), 0)
    lowest = position // 2 == levels - 1
    lat_inside = (lat >= region_smem[0]) & (lat < region_smem[1]) & lowest
    score = jnp.sum(
        jnp.where(lat_inside, weights, 0.0) * jnp.sum(region_sum, axis=1, keepdims=True),
        axis=0,
        keepdims=True,
    )
    score = jnp.broadcast_to(score, (waves, LANES))
    high = score.astype(jnp.bfloat16).astype(jnp.float32)
    middle = (score - high).astype(jnp.bfloat16).astype(jnp.float32)
    low = score - high - middle
    lane = lax.broadcasted_iota(jnp.int32, score.shape, 1)
    parts = jnp.where(lane == 0, high, jnp.where(lane == 1, middle, jnp.where(lane == 2, low, 0.0)))
    out_ref[:, 2 * every :] = parts.astype(jnp.bfloat16)
    row = lax.broadcasted_iota(jnp.int32, (every, 1), 0)
    scale = jnp.where(row < lats, 0.5 * analysis_scale, analysis_scale)
    for part in range(2):
        out_ref[:, part * every : (part + 1) * every] = (
            (scale * total_ref[:, part * waves : (part + 1) * waves]).astype(jnp.bfloat16).T
        )


def to_degrees(
    levels,
    waves_total,
    region_smem,
    coef_ref,
    legendre_ref,
    state_ref,
    lat_weights_ref,
    out_ref,
    scores_ref,
    wide_ref,
):
    waves, degrees, lats = legendre_ref.shape
    owners = coef_ref.shape[0]
    half = lats // 2
    span = lats // LANES
    parts = jnp.zeros((1, LANES), jnp.float32)
    for owner in range(owners):
        values = coef_ref[owner].astype(jnp.float32)
        put_rows(wide_ref, 0, pl.ds(owner * waves, waves), values[:, : 2 * lats])
        parts += values[0:1, 2 * lats :]
    lat = lax.broadcasted_iota(jnp.int32, (1, lats), 1)
    inside = (lat >= region_smem[0]) & (lat < region_smem[1])
    weight = jnp.sum(jnp.where(inside, lat_weights_ref[...].reshape(1, lats), 0.0), axis=1, keepdims=True)
    columns = (region_smem[3] - region_smem[2]).astype(jnp.float32)
    scores_ref[...] = jnp.sum(parts, axis=1, keepdims=True) / (weight * columns)

    position = lax.axis_index("wave")
    degree = lax.broadcasted_iota(jnp.int32, (1, degrees), 1).astype(jnp.float32)
    undamped = 1.0 / (1.0 + ((degree + 1.0) / degrees) ** 2)
    left = lax.broadcasted_iota(jnp.int32, (levels, lats), 1) < half
    middle = 2 * levels
    for wave in range(waves):
        rows = []
        for part in range(2):
            first = get_rows(wide_ref, part * span, span, pl.ds(wave, levels, stride=2 * waves))
            second = get_rows(wide_ref, part * span, span, pl.ds(waves + wave, levels, stride=2 * waves))
            rows.append(jnp.where(left, first, pltpu.roll(second, half, 1)))
            rows.append(jnp.where(left, pltpu.roll(first, half, 1), second))
        tendency = lax.dot_general(
            legendre_ref[wave],
            jnp.concatenate(rows, axis=0).astype(jnp.bfloat16),
            (((1,), (1,)), ((), ())),
            preferred_element_type=jnp.float32,
        ).T
        global_wave = (position * waves + wave).astype(jnp.float32)
        advection = advect_rate * global_wave / waves_total
        out_ref[wave, :middle] = (
            (state_ref[wave, :middle] + advection * tendency[middle:]) * undamped
        ).astype(jnp.bfloat16)
        out_ref[wave, middle:] = (
            (state_ref[wave, middle:] - advection * tendency[:middle]) * undamped
        ).astype(jnp.bfloat16)


def pick(sources_smem, pieces_ref, out_ref):
    for slot in range(out_ref.shape[0]):
        out_ref[slot] = pieces_ref[sources_smem[slot]]


def on_device(state, legendre, lat_weights, region, sources):
    wave_count = lax.axis_size("wave")
    member_count = lax.axis_size("member")
    waves_local, degrees, latitudes = legendre.shape
    waves_total = waves_local * wave_count
    state_rows = state.shape[2]
    levels = state_rows // 4
    spectral = state[0]
    lat_row = lat_weights
    whole = pl.BlockSpec(memory_space=pltpu.VMEM)
    scalars = pl.BlockSpec(memory_space=pltpu.SMEM)
    stay = pl.BlockSpec(memory_space=pltpu.HBM)
    small = pltpu.CompilerParams(vmem_limit_bytes=16 << 20)
    near = [
        pltpu.VMEM(legendre.shape, jnp.bfloat16),
        pltpu.VMEM(spectral.shape, jnp.float32),
    ]
    arrivals = [pltpu.SemaphoreType.DMA((waves_local,)), pltpu.SemaphoreType.DMA((waves_local,))]

    coef, fourier, legendre_near, spectral_near = pl.pallas_call(
        functools.partial(to_latitudes, levels),
        in_specs=[stay, stay],
        out_specs=[whole, whole, whole, whole],
        out_shape=[
            pltpu.VMEM((wave_count, waves_local, 2 * latitudes), jnp.bfloat16),
            pltpu.VMEM((2 * waves_total, NLON), jnp.bfloat16),
            pltpu.VMEM(legendre.shape, jnp.bfloat16),
            pltpu.VMEM(spectral.shape, jnp.float32),
        ],
        scratch_shapes=[
            pltpu.VMEM((latitudes // LANES, waves_local * state_rows, LANES), jnp.float32),
            *arrivals,
        ],
        compiler_params=pltpu.CompilerParams(vmem_limit_bytes=52 << 20),
        name="to_latitudes",
    )(spectral, legendre)
    coef = lax.all_to_all(coef, "wave", split_axis=0, concat_axis=0, tiled=True)

    width = 2 * latitudes + LANES
    flux_coef = pl.pallas_call(
        functools.partial(on_grid, (2.0 * waves_total) ** (-0.5), NLON ** (-0.5), levels),
        in_specs=[scalars, whole, whole, whole],
        out_specs=whole,
        out_shape=jax.ShapeDtypeStruct((waves_total, width), jnp.bfloat16),
        scratch_shapes=[
            pltpu.VMEM((latitudes, 8), jnp.float32),
            pltpu.VMEM((latitudes, 2 * waves_total), jnp.bfloat16),
            pltpu.VMEM((latitudes, 2 * waves_total), jnp.float32),
        ],
        compiler_params=small,
        name="on_grid",
    )(region, coef.reshape(waves_total, 2 * latitudes), fourier, lat_row)
    flux_coef = lax.all_to_all(
        flux_coef.reshape(wave_count, waves_local, width), "wave", split_axis=0, concat_axis=0, tiled=True
    )

    stepped, scores = pl.pallas_call(
        functools.partial(to_degrees, levels, waves_total),
        in_specs=[scalars, whole, whole, whole, whole],
        out_specs=[whole, whole],
        out_shape=[
            jax.ShapeDtypeStruct((waves_local, state_rows, degrees), jnp.bfloat16),
            jax.ShapeDtypeStruct((1, 1), jnp.float32),
        ],
        scratch_shapes=[
            pltpu.VMEM((2 * latitudes // LANES, wave_count * waves_local, LANES), jnp.float32)
        ],
        compiler_params=small,
        name="to_degrees",
    )(region, flux_coef, legendre_near, spectral_near, lat_row)

    piece_rows = waves_local * state_rows // member_count
    pieces = lax.all_to_all(
        stepped.reshape(member_count, piece_rows, degrees),
        "member",
        split_axis=0,
        concat_axis=0,
        tiled=True,
    )
    picked = pl.pallas_call(
        pick,
        in_specs=[scalars, whole],
        out_specs=whole,
        out_shape=jax.ShapeDtypeStruct(pieces.shape, jnp.bfloat16),
        compiler_params=small,
        name="pick",
    )(sources, pieces)
    cloned = lax.all_to_all(picked, "member", split_axis=0, concat_axis=0, tiled=True)
    cloned = cloned.reshape(1, waves_local, state_rows, degrees).astype(jnp.float32)
    return (cloned, scores.reshape(1))


def solution(mesh):
    in_specs = (P("member", "wave", None, None), P("wave", None, None), P(), P(), P())
    out_specs = (P("member", "wave", None, None), P("member"))
    return jax.shard_map(
        on_device, mesh=mesh, in_specs=in_specs, out_specs=out_specs, check_vma=False
    )
```

```python
import functools

import jax
import jax.numpy as jnp
from jax import lax
from jax.experimental import pallas as pl
from jax.experimental.pallas import tpu as pltpu
from jax.sharding import PartitionSpec as P

NLON = 2560
LANES = 128
COLUMNS = 256
AHEAD = 8

advect_rate = 2.0


def put_rows(tiles_ref, first_tile, where, values):
    for tile in range(values.shape[1] // LANES):
        tiles_ref[first_tile + tile, where, :] = values[:, tile * LANES : (tile + 1) * LANES]


def get_rows(tiles_ref, first_tile, tiles, where):
    return jnp.concatenate([tiles_ref[first_tile + tile, where, :] for tile in range(tiles)], axis=1)


def routes(waves, *pairs):
    copies = [
        [pltpu.make_async_copy(far.at[wave], near.at[wave], sems.at[wave]) for far, near, sems in pairs]
        for wave in range(waves)
    ]
    for group in copies[:AHEAD]:
        for copy in group:
            copy.start()
    return copies


def arrive(copies, wave):
    for copy in copies[wave]:
        copy.wait()
    for copy in copies[wave + AHEAD] if wave + AHEAD < len(copies) else ():
        copy.start()


def turns(row_steps, column_steps, shift, points):
    steps = row_steps * column_steps + shift
    steps = steps - jnp.floor(steps * (1.0 / points)) * points
    return steps * (2.0 * jnp.pi / points)


def to_latitudes(
    levels,
    state_hbm,
    legendre_hbm,
    out_ref,
    fourier_ref,
    legendre_ref,
    state_ref,
    rows_ref,
    state_sems,
    legendre_sems,
):
    waves, rows, _ = state_hbm.shape
    halves = [pl.ds(part * (legendre_hbm.shape[1] // 2), legendre_hbm.shape[1] // 2) for part in range(2)]
    copies = routes(
        waves,
        (state_hbm, state_ref, state_sems),
        *(
            (legendre_hbm.at[:, here], legendre_ref.at[:, here], legendre_sems.at[part])
            for part, here in enumerate(halves)
        ),
    )
    table_rows, points = fourier_ref.shape
    total = table_rows // 2
    row = lax.broadcasted_iota(jnp.int32, (table_rows, LANES), 0)
    lane = lax.broadcasted_iota(jnp.int32, (table_rows, LANES), 1).astype(jnp.float32)
    quarter = jnp.where(row >= total, points // 4, 0).astype(jnp.float32)
    order = jnp.where(row >= total, row - total, row).astype(jnp.float32)
    coarse = turns(order, lane * LANES, quarter, points)
    fine = turns(order[:total], lane[:total], 0.0, points)
    cos_coarse, sin_coarse = jnp.cos(coarse), jnp.sin(coarse)
    cos_fine, sin_fine = jnp.cos(fine), jnp.sin(fine)
    tiles = points // LANES
    for wave in range(waves):
        arrive(copies, wave)
        product = jnp.dot(
            state_ref[wave].astype(jnp.bfloat16),
            legendre_ref[wave],
            preferred_element_type=jnp.float32,
        )
        put_rows(rows_ref, 0, pl.ds(wave, rows, stride=waves), product)
        for tile in range(wave * tiles // waves, (wave + 1) * tiles // waves):
            for part in range(2):
                here = slice(part * total, (part + 1) * total)
                fourier_ref[here, tile * LANES : (tile + 1) * LANES] = (
                    cos_coarse[here, tile : tile + 1] * cos_fine
                    - sin_coarse[here, tile : tile + 1] * sin_fine
                ).astype(jnp.bfloat16)
    width = out_ref.shape[2] // 2
    half = width // 2
    span = width // LANES
    left = lax.broadcasted_iota(jnp.int32, (waves, width), 1) < half
    for level in range(levels):
        for part in range(2):
            first = 2 * levels * part + level
            wind = get_rows(rows_ref, 0, span, pl.ds(first * waves, waves))
            temper = get_rows(rows_ref, 0, span, pl.ds((first + levels) * waves, waves))
            low = jnp.where(left, wind, pltpu.roll(temper, half, 1))
            high = jnp.where(left, pltpu.roll(wind, half, 1), temper)
            here = slice(part * width, (part + 1) * width)
            out_ref[2 * level, :, here] = low.astype(jnp.bfloat16)
            out_ref[2 * level + 1, :, here] = high.astype(jnp.bfloat16)


def on_grid(
    synthesis_scale,
    analysis_scale,
    levels,
    region_smem,
    coef_ref,
    fourier_ref,
    lat_weights_ref,
    out_ref,
    weights_ref,
    turned_ref,
    total_ref,
):
    points = fourier_ref.shape[1]
    every = lat_weights_ref.shape[0]
    lats = every // 2
    waves = coef_ref.shape[0]
    position = lax.axis_index("wave")
    lat_start = pl.multiple_of((position % 2) * lats, 8)
    weights_ref[...] = jnp.broadcast_to(lat_weights_ref[...].reshape(1, every), (8, every)).T
    weights = weights_ref[pl.ds(lat_start, lats), 0:1] * (synthesis_scale * synthesis_scale)
    for part in range(2):
        turned_ref[:, part * waves : (part + 1) * waves] = coef_ref[:, part * every : (part + 1) * every].T
    region_sum = jnp.zeros((lats, LANES), jnp.float32)
    for part in range(points // COLUMNS):
        table = fourier_ref[:, part * COLUMNS : (part + 1) * COLUMNS]
        grid = jnp.dot(turned_ref[...], table, preferred_element_type=jnp.float32)
        wind, temper = grid[:lats], grid[lats:]
        weighted = wind * weights
        for rows, flux in ((slice(0, lats), wind * weighted), (slice(lats, every), weighted * temper)):
            term = lax.dot_general(
                flux.astype(jnp.bfloat16),
                table,
                (((1,), (1,)), ((), ())),
                preferred_element_type=jnp.float32,
            )
            total_ref[rows] = term if part == 0 else total_ref[rows] + term
        column = part * COLUMNS + lax.broadcasted_iota(jnp.int32, (1, COLUMNS), 1)
        inside = (column >= region_smem[2]) & (column < region_smem[3])
        squares = jnp.where(inside, temper * temper, 0.0)
        for tile in range(COLUMNS // LANES):
            region_sum += squares[:, tile * LANES : (tile + 1) * LANES]
    lat = lat_start + lax.broadcasted_iota(jnp.int32, (lats, 1), 0)
    lowest = position // 2 == levels - 1
    lat_inside = (lat >= region_smem[0]) & (lat < region_smem[1]) & lowest
    score = jnp.sum(
        jnp.where(lat_inside, weights, 0.0) * jnp.sum(region_sum, axis=1, keepdims=True),
        axis=0,
        keepdims=True,
    )
    score = jnp.broadcast_to(score, (waves, LANES))
    high = score.astype(jnp.bfloat16).astype(jnp.float32)
    middle = (score - high).astype(jnp.bfloat16).astype(jnp.float32)
    low = score - high - middle
    lane = lax.broadcasted_iota(jnp.int32, score.shape, 1)
    parts = jnp.where(lane == 0, high, jnp.where(lane == 1, middle, jnp.where(lane == 2, low, 0.0)))
    out_ref[:, 2 * every :] = parts.astype(jnp.bfloat16)
    row = lax.broadcasted_iota(jnp.int32, (every, 1), 0)
    scale = jnp.where(row < lats, 0.5 * analysis_scale, analysis_scale)
    for part in range(2):
        out_ref[:, part * every : (part + 1) * every] = (
            (scale * total_ref[:, part * waves : (part + 1) * waves]).astype(jnp.bfloat16).T
        )


def to_degrees(
    levels,
    waves_total,
    region_smem,
    coef_ref,
    legendre_ref,
    state_ref,
    lat_weights_ref,
    out_ref,
    scores_ref,
    wide_ref,
):
    waves, degrees, lats = legendre_ref.shape
    owners = coef_ref.shape[0]
    half = lats // 2
    span = lats // LANES
    parts = jnp.zeros((1, LANES), jnp.float32)
    for owner in range(owners):
        values = coef_ref[owner].astype(jnp.float32)
        put_rows(wide_ref, 0, pl.ds(owner * waves, waves), values[:, : 2 * lats])
        parts += values[0:1, 2 * lats :]
    lat = lax.broadcasted_iota(jnp.int32, (1, lats), 1)
    inside = (lat >= region_smem[0]) & (lat < region_smem[1])
    weight = jnp.sum(jnp.where(inside, lat_weights_ref[...].reshape(1, lats), 0.0), axis=1, keepdims=True)
    columns = (region_smem[3] - region_smem[2]).astype(jnp.float32)
    scores_ref[...] = jnp.sum(parts, axis=1, keepdims=True) / (weight * columns)

    position = lax.axis_index("wave")
    degree = lax.broadcasted_iota(jnp.int32, (1, degrees), 1).astype(jnp.float32)
    undamped = 1.0 / (1.0 + ((degree + 1.0) / degrees) ** 2)
    left = lax.broadcasted_iota(jnp.int32, (levels, lats), 1) < half
    middle = 2 * levels
    for wave in range(waves):
        rows = []
        for part in range(2):
            first = get_rows(wide_ref, part * span, span, pl.ds(wave, levels, stride=2 * waves))
            second = get_rows(wide_ref, part * span, span, pl.ds(waves + wave, levels, stride=2 * waves))
            rows.append(jnp.where(left, first, pltpu.roll(second, half, 1)))
            rows.append(jnp.where(left, pltpu.roll(first, half, 1), second))
        tendency = lax.dot_general(
            legendre_ref[wave],
            jnp.concatenate(rows, axis=0).astype(jnp.bfloat16),
            (((1,), (1,)), ((), ())),
            preferred_element_type=jnp.float32,
        ).T
        global_wave = (position * waves + wave).astype(jnp.float32)
        advection = advect_rate * global_wave / waves_total
        out_ref[wave, :middle] = (
            (state_ref[wave, :middle] + advection * tendency[middle:]) * undamped
        ).astype(jnp.bfloat16)
        out_ref[wave, middle:] = (
            (state_ref[wave, middle:] - advection * tendency[:middle]) * undamped
        ).astype(jnp.bfloat16)


def pick(sources_smem, pieces_ref, out_ref):
    for slot in range(out_ref.shape[0]):
        out_ref[slot] = pieces_ref[sources_smem[slot]]


def on_device(state, legendre, lat_weights, region, sources):
    wave_count = lax.axis_size("wave")
    member_count = lax.axis_size("member")
    waves_local, degrees, latitudes = legendre.shape
    waves_total = waves_local * wave_count
    state_rows = state.shape[2]
    levels = state_rows // 4
    spectral = state[0]
    lat_row = lat_weights
    whole = pl.BlockSpec(memory_space=pltpu.VMEM)
    scalars = pl.BlockSpec(memory_space=pltpu.SMEM)
    stay = pl.BlockSpec(memory_space=pltpu.HBM)
    small = pltpu.CompilerParams(vmem_limit_bytes=16 << 20)
    near = [
        pltpu.VMEM(legendre.shape, jnp.bfloat16),
        pltpu.VMEM(spectral.shape, jnp.float32),
    ]
    arrivals = [pltpu.SemaphoreType.DMA((waves_local,)), pltpu.SemaphoreType.DMA((2, waves_local))]

    coef, fourier, legendre_near = pl.pallas_call(
        functools.partial(to_latitudes, levels),
        in_specs=[stay, stay],
        out_specs=[whole, whole, whole],
        out_shape=[
            pltpu.VMEM((wave_count, waves_local, 2 * latitudes), jnp.bfloat16),
            pltpu.VMEM((2 * waves_total, NLON), jnp.bfloat16),
            pltpu.VMEM(legendre.shape, jnp.bfloat16),
        ],
        scratch_shapes=[
            pltpu.VMEM(spectral.shape, jnp.float32),
            pltpu.VMEM((latitudes // LANES, waves_local * state_rows, LANES), jnp.float32),
            *arrivals,
        ],
        compiler_params=pltpu.CompilerParams(vmem_limit_bytes=52 << 20),
        name="to_latitudes",
    )(spectral, legendre)
    coef = lax.all_to_all(coef, "wave", split_axis=0, concat_axis=0, tiled=True)

    width = 2 * latitudes + LANES
    flux_coef = pl.pallas_call(
        functools.partial(on_grid, (2.0 * waves_total) ** (-0.5), NLON ** (-0.5), levels),
        in_specs=[scalars, whole, whole, whole],
        out_specs=whole,
        out_shape=jax.ShapeDtypeStruct((waves_total, width), jnp.bfloat16),
        scratch_shapes=[
            pltpu.VMEM((latitudes, 8), jnp.float32),
            pltpu.VMEM((latitudes, 2 * waves_total), jnp.bfloat16),
            pltpu.VMEM((latitudes, 2 * waves_total), jnp.float32),
        ],
        compiler_params=small,
        name="on_grid",
    )(region, coef.reshape(waves_total, 2 * latitudes), fourier, lat_row)
    flux_coef = lax.all_to_all(
        flux_coef.reshape(wave_count, waves_local, width), "wave", split_axis=0, concat_axis=0, tiled=True
    )

    stepped, scores = pl.pallas_call(
        functools.partial(to_degrees, levels, waves_total),
        in_specs=[scalars, whole, whole, whole, whole],
        out_specs=[whole, whole],
        out_shape=[
            jax.ShapeDtypeStruct((waves_local, state_rows, degrees), jnp.bfloat16),
            jax.ShapeDtypeStruct((1, 1), jnp.float32),
        ],
        scratch_shapes=[
            pltpu.VMEM((2 * latitudes // LANES, wave_count * waves_local, LANES), jnp.float32)
        ],
        compiler_params=small,
        name="to_degrees",
    )(region, flux_coef, legendre_near, spectral, lat_row)

    piece_rows = waves_local * state_rows // member_count
    pieces = lax.all_to_all(
        stepped.reshape(member_count, piece_rows, degrees),
        "member",
        split_axis=0,
        concat_axis=0,
        tiled=True,
    )
    picked = pl.pallas_call(
        pick,
        in_specs=[scalars, whole],
        out_specs=whole,
        out_shape=jax.ShapeDtypeStruct(pieces.shape, jnp.bfloat16),
        compiler_params=small,
        name="pick",
    )(sources, pieces)
    cloned = lax.all_to_all(picked, "member", split_axis=0, concat_axis=0, tiled=True)
    cloned = cloned.reshape(1, waves_local, state_rows, degrees).astype(jnp.float32)
    return (cloned, scores.reshape(1))


def solution(mesh):
    in_specs = (P("member", "wave", None, None), P("wave", None, None), P(), P(), P())
    out_specs = (P("member", "wave", None, None), P("member"))
    return jax.shard_map(
        on_device, mesh=mesh, in_specs=in_specs, out_specs=out_specs, check_vma=False
    )
```
